256 devices in a mesh: pipe: 4 (over y_lo, core), ctx: 16 (over z, y_hi), tp: 4 (over x).
Axes of the slice: x: 4, y: 4 (y_hi: 2, y_lo: 2; y = y_hi * 2 + y_lo), z: 8, core: 2. Of those that a mesh axis runs over, the one named last changes fastest.
Arguments:
- segment_inputs: bfloat16 [4, 2, 2048, 4096], P('pipe', None, ('ctx', 'tp')), may hold values from -128 to 128
- keys: bfloat16 [4, 2, 2048, 512], P('pipe', None, 'ctx', 'tp'), may hold values from -64 to 64
- values: bfloat16 [4, 2, 2048, 512], P('pipe', None, 'ctx', 'tp'), may hold values from -6 to 6
- norm_gain: float32 [4, 4096], P('pipe'), may hold values from 0.1 to 1.9
- waiting_grads: bfloat16 [4, 2048, 4096], P('pipe', ('ctx', 'tp')), may hold values from -32 to 32
- output_grads: bfloat16 [1, 2048, 4096], P(None, ('ctx', 'tp')), may hold values from -32 to 32
- doc_lengths: int32 [5, 8], replicated, may hold values from 1 to 1024, as said below
Outputs:
- input_grads: bfloat16 [4, 2, 2048, 4096], P('pipe', None, ('ctx', 'tp'))
- key_grads: float32 [4, 2, 2048, 512], P('pipe', None, 'ctx', 'tp')
- value_grads: float32 [4, 2, 2048, 512], P('pipe', None, 'ctx', 'tp')
- gain_grads: float32 [4, 4096], P('pipe')
The draws below stay inside these ranges and needn't reach their ends.
Inputs may be any that keep to these rules, and one draw needn't show every extreme that they name: `doc_lengths`: row m lists in order of position the lengths of the 8 documents packed into microbatch m's sequence; each row sums to 2048; the last document is exactly 1024 long.
All inputs are finite; a program needn't handle non-finite values.
Results may differ from the reference program's by a relative error of at most 0.009.
The reference program's roundings to bfloat16 on the way (of `queries`, `arriving`, `dscore`, `probs_low` and `query_grad`) count: a program that leaves them out, or rounds other values in their place, can miss the bound.
Values may be sent and summed in bfloat16 or wider, within the bound.
A program may use at most 64 MiB of HBM per device.

```python
import jax
import jax.numpy as jnp
from jax import lax

QH = 32
KVH = 4
HD = 128
S_DEV = 128
TICKS = 2
DOCS = 8
SEGMENTS = 4
MICRO = 5
SEQ = 2048
QW = 4096
KVW = 512
DOC_MOST = 1024
N_CTX = 16


def input_field(key):
    full_shape = (SEGMENTS, TICKS, SEQ, QW)
    key_core, key_cols, key_rows = jax.random.split(jax.random.fold_in(key, 101), 3)
    col_scale = 10.0 ** jax.random.uniform(key_cols, (SEGMENTS, 1, 1, QW), jnp.float32)
    row_scale = 10.0 ** (jax.random.uniform(key_rows, (SEGMENTS, TICKS, SEQ, 1), jnp.float32) - 0.5)
    core_draw = jnp.clip(jax.random.normal(key_core, full_shape, jnp.float32), -4.0, 4.0)
    return core_draw * col_scale * row_scale


def draw_segment_inputs(key, part):
    return input_field(key).astype(jnp.bfloat16)


def draw_keys(key, part):
    full_shape = (SEGMENTS, TICKS, SEQ, KVW)
    key_base = jax.random.fold_in(jax.random.fold_in(key, 202), 0)
    base_draw = jnp.clip(jax.random.normal(key_base, full_shape, jnp.float32), -4.0, 4.0)
    return base_draw.astype(jnp.bfloat16)


def grad_field(key, lead_count, salt_value):
    full_shape = (lead_count, SEQ, QW)
    key_core, key_rows = jax.random.split(jax.random.fold_in(key, salt_value), 2)
    position = jnp.arange(SEQ, dtype=jnp.float32) / SEQ - 0.5
    growth = 3.0
    row_trend = (growth ** position)[None, :, None]
    spread = 10.0 ** (jax.random.uniform(key_rows, (lead_count, SEQ, 1), jnp.float32) - 0.5)
    core_draw = jnp.clip(jax.random.normal(key_core, full_shape, jnp.float32), -4.0, 4.0)
    return core_draw * row_trend * spread


def draw_waiting_grads(key, part):
    return grad_field(key, SEGMENTS, 303).astype(jnp.bfloat16)


def draw_output_grads(key, part):
    return grad_field(key, TICKS - 1, 404).astype(jnp.bfloat16)


def draw_doc_lengths(key, part):
    remaining = SEQ - DOC_MOST

    def one_row(row_key):
        picked = jax.random.permutation(row_key, remaining - 1)[:DOCS - 2] + 1
        cuts = jnp.sort(picked.astype(jnp.int32))
        edges = jnp.concatenate([jnp.zeros((1,), jnp.int32), cuts, jnp.full((1,), remaining, jnp.int32)])
        return jnp.concatenate([edges[1:] - edges[:-1], jnp.full((1,), DOC_MOST, jnp.int32)])
    return jax.vmap(one_row)(jax.random.split(jax.random.fold_in(key, 505), MICRO))


def shard_levels(stream_key, shape, cuts, low, high):
    level, own = 1.0, jax.random.fold_in(stream_key, 6)
    for dim, parts in cuts:
        draws = jnp.exp(jax.random.uniform(jax.random.fold_in(own, dim), (parts,), jnp.float32, low / len(cuts), high / len(cuts)))
        level = level * jnp.repeat(draws, shape[dim] // parts).reshape([-1 if axis == dim else 1 for axis in range(len(shape))])
    return level


def centred(rng, shape, scale, limit, pieces=(), kind=jnp.bfloat16):
    array = scale * jax.random.normal(rng, shape, jnp.float32)
    if pieces:
        array = array * shard_levels(rng, shape, pieces, -0.22, 0.18)
    return jnp.clip(array, -limit, limit).astype(kind)


def setup_inputs(seed: int = 0) -> dict:
    splits = jax.random.split(jax.random.key(seed), 8)
    segment_inputs = draw_segment_inputs(jax.random.fold_in(splits[7], 71), 0)
    keys = draw_keys(jax.random.fold_in(splits[7], 71), 0)
    values = centred(splits[2], (SEGMENTS, TICKS, SEQ, KVW), 1.0, 6.0, ((0, 4), (2, 16), (3, 4)))
    norm_gain = jnp.clip(1.0 + 0.18 * jax.random.normal(splits[3], (SEGMENTS, QW), jnp.float32), 0.1, 1.9)
    waiting_grads = draw_waiting_grads(jax.random.fold_in(splits[7], 71), 0)
    output_grads = draw_output_grads(jax.random.fold_in(splits[7], 71), 0)
    doc_lengths = draw_doc_lengths(jax.random.fold_in(splits[7], 71), 0)
    return dict(segment_inputs=segment_inputs, keys=keys, values=values, norm_gain=norm_gain, waiting_grads=waiting_grads, output_grads=output_grads, doc_lengths=doc_lengths)


epsilon = 1e-05
masked_fill = -1e+30

def row_positions(rows, half_rows, cycle_count):
    section = rows // half_rows
    offset = rows % half_rows
    owner = section // 2
    placed = jnp.where(section % 2 == 0, owner, 2 * cycle_count - 1 - owner)
    return (placed * half_rows + offset).astype(jnp.int32)

def document_starts(lengths_row, positions):
    closing = jnp.cumsum(lengths_row)
    passed = closing[None, :] <= positions[:, None]
    return lax.optimization_barrier(jnp.sum(jnp.where(passed, lengths_row[None, :], 0), axis=1)).astype(jnp.int32)

def segment_tick(inputs, key_rows, value_rows, gain_row, arriving, lengths_row):
    scale_factor = HD ** (-0.5)
    group_size = QH // KVH
    widened = inputs.astype(jnp.float32)
    inverse = lax.rsqrt(lax.optimization_barrier(jnp.mean(widened * widened, axis=-1, keepdims=True)) + epsilon)
    normed = widened * inverse
    queries = (normed * gain_row[None, :]).astype(jnp.bfloat16)
    positions = row_positions(jnp.arange(SEQ, dtype=jnp.int32), S_DEV // 2, N_CTX)
    starts = document_starts(lengths_row, positions)
    visible = (positions[None, :] <= positions[:, None]) & (positions[None, :] >= starts[:, None])

    def one_head(head_index):
        shared = head_index // group_size
        query_head = lax.dynamic_slice_in_dim(queries, head_index * HD, HD, 1)
        grad_head = lax.dynamic_slice_in_dim(arriving, head_index * HD, HD, 1)
        key_head = lax.dynamic_slice_in_dim(key_rows, shared * HD, HD, 1)
        value_head = lax.dynamic_slice_in_dim(value_rows, shared * HD, HD, 1)
        scores = scale_factor * jnp.dot(query_head, key_head.T, preferred_element_type=jnp.float32)
        filled = jnp.where(visible, scores, masked_fill)
        row_peak = lax.optimization_barrier(jnp.max(filled, axis=-1, keepdims=True))
        row_total = lax.optimization_barrier(jnp.sum(jnp.where(visible, jnp.exp(scores - row_peak), 0.0), axis=-1, keepdims=True))
        logsum = row_peak + jnp.log(row_total)
        prob_weights = jnp.where(visible, jnp.exp(scores - logsum), 0.0)
        prob_grad = jnp.dot(grad_head, value_head.T, preferred_element_type=jnp.float32)
        row_term = lax.optimization_barrier(jnp.sum(prob_weights * prob_grad, axis=-1, keepdims=True))
        dscore = (prob_weights * (prob_grad - row_term)).astype(jnp.bfloat16)
        probs_low = prob_weights.astype(jnp.bfloat16)
        dquery = scale_factor * jnp.dot(dscore, key_head, preferred_element_type=jnp.float32)
        key_grad = scale_factor * jnp.dot(dscore.T, query_head, preferred_element_type=jnp.float32)
        dvalue = jnp.dot(probs_low.T, grad_head, preferred_element_type=jnp.float32)
        return (dquery, key_grad, dvalue)
    dquery, key_grad, dvalue = lax.map(one_head, jnp.arange(QH, dtype=jnp.int32))
    query_grad = jnp.transpose(dquery, (1, 0, 2)).reshape(SEQ, QW)
    key_sum = lax.optimization_barrier(jnp.sum(key_grad.reshape(KVH, group_size, SEQ, HD), axis=1))
    value_sum = lax.optimization_barrier(jnp.sum(dvalue.reshape(KVH, group_size, SEQ, HD), axis=1))
    key_out = jnp.transpose(key_sum, (1, 0, 2)).reshape(SEQ, KVW)
    value_out = jnp.transpose(value_sum, (1, 0, 2)).reshape(SEQ, KVW)
    rounded = lax.optimization_barrier(query_grad.astype(jnp.bfloat16)).astype(jnp.float32)
    scaled = rounded * gain_row[None, :]
    coupling = lax.optimization_barrier(jnp.mean(scaled * normed, axis=-1, keepdims=True))
    input_grad = (arriving.astype(jnp.float32) + inverse * (scaled - normed * coupling)).astype(jnp.bfloat16)
    gain_part = lax.optimization_barrier(jnp.sum(rounded * normed, axis=0))
    return (input_grad, key_out, value_out, gain_part)

def reference(segment_inputs, keys, values, norm_gain, waiting_grads, output_grads, doc_lengths):
    results = {}
    for tick_index in range(TICKS):
        for segment_index in range(SEGMENTS):
            if tick_index == 0:
                arriving = waiting_grads[segment_index]
            elif segment_index == SEGMENTS - 1:
                arriving = output_grads[tick_index - 1]
            else:
                arriving = results[segment_index + 1, tick_index - 1][0]
            lengths_row = doc_lengths[segment_index + tick_index]
            results[segment_index, tick_index] = segment_tick(segment_inputs[segment_index, tick_index], keys[segment_index, tick_index], values[segment_index, tick_index], norm_gain[segment_index], arriving, lengths_row)
    input_grads = jnp.stack([jnp.stack([results[segment_index, tick_index][0] for tick_index in range(TICKS)]) for segment_index in range(SEGMENTS)])
    key_grads = jnp.stack([jnp.stack([results[segment_index, tick_index][1] for tick_index in range(TICKS)]) for segment_index in range(SEGMENTS)])
    value_grads = jnp.stack([jnp.stack([results[segment_index, tick_index][2] for tick_index in range(TICKS)]) for segment_index in range(SEGMENTS)])
    gain_rows = []
    for segment_index in range(SEGMENTS):
        running = jnp.zeros((QW,), jnp.float32)
        for tick_index in range(TICKS):
            running = running + results[segment_index, tick_index][3]
        gain_rows.append(running)
    gain_grads = jnp.stack(gain_rows)
    return (input_grads, key_grads, value_grads, gain_grads)
```

```python
import functools
import math

import jax
import jax.numpy as jnp
from jax import lax
from jax.experimental import pallas as pl
from jax.experimental.pallas import tpu as pltpu
from jax.sharding import PartitionSpec as P

HD = 128
HALF = 64
EPS = 1e-05
MASKED = -1e30
SCALE = HD ** (-0.5)
EXP2_SCALE = SCALE * math.log2(math.e)
MESH = pl.DeviceIdType.MESH
f32 = jnp.float32
bf16 = jnp.bfloat16


def remote(src, dst, send_sem, recv_sem, device):
    return pltpu.make_async_remote_copy(
        src_ref=src,
        dst_ref=dst,
        send_sem=send_sem,
        recv_sem=recv_sem,
        device_id=device,
        device_id_type=MESH,
    )


def dot_nt(a, b):
    return lax.dot_general(a, b, (((1,), (1,)), ((), ())), preferred_element_type=f32)


def dot_tn(a, b):
    return lax.dot_general(a, b, (((0,), (0,)), ((), ())), preferred_element_type=f32)


def kernel(
    dims,
    x_hbm,
    k_hbm,
    v_hbm,
    gain_ref,
    w_hbm,
    og_hbm,
    doc_ref,
    ig_out,
    dk_out,
    dv_out,
    gain_out,
    xrow,
    xh,
    ah,
    invh,
    kb,
    vb,
    qs,
    dos,
    e_ref,
    dp_ref,
    m_ref,
    l_ref,
    w_ref,
    rt_ref,
    dqt,
    dqs,
    dkf,
    dvf,
    dks,
    dvs,
    gk,
    gv,
    ig,
    cs,
    cr,
    gacc,
    gr,
    dko,
    dvo,
    local_sem,
    x_s,
    x_r,
    a_s,
    a_r,
    inv_s,
    inv_r,
    k_s,
    k_r,
    v_s,
    v_r,
    dk_s,
    dk_r,
    dv_s,
    dv_r,
    c_s,
    c_r,
    p_s,
    p_r,
    o_s,
    o_r,
    g_s,
    g_r,
    h_s,
    h_r,
):
    n_pipe, n_ctx, n_tp, ticks, group, docs = dims
    n = n_ctx
    rows = 2 * HALF // n_tp
    cols = group * HD
    width = n_tp * cols
    lanes = group * HALF
    chunk = 256
    pairs = (n + 2) // 2

    seg = lax.axis_index("pipe")
    me = lax.axis_index("ctx")
    tp = lax.axis_index("tp")
    last = n_pipe - 1
    low_pairs = (me + 2) // 2
    high_first = 2 * low_pairs

    def ctx_peer(d):
        return lax.rem(me + d, n)

    def ctx_behind(d):
        return lax.rem(me + n - d, n)

    def tp_peer(d):
        return lax.rem(tp + d, n_tp)

    def slot_of(d):
        wrapped = (n + d - 1 - me) // n
        return (1 - wrapped) * d + wrapped * (high_first + n - d)

    barrier = pltpu.get_barrier_semaphore()

    @pl.loop(1, n)
    def _(d):
        pl.semaphore_signal(barrier, inc=1, device_id={"ctx": ctx_peer(d)}, device_id_type=MESH)

    for d in range(1, n_tp):
        pl.semaphore_signal(barrier, inc=1, device_id={"tp": tp_peer(d)}, device_id_type=MESH)
    pl.semaphore_signal(
        barrier, inc=1, device_id={"pipe": lax.rem(seg + 1, n_pipe)}, device_id_type=MESH
    )
    pl.semaphore_signal(
        barrier, inc=1, device_id={"pipe": lax.rem(seg + n_pipe - 1, n_pipe)}, device_id_type=MESH
    )

    own_rows = pl.ds(pl.multiple_of(tp * rows, rows), rows)
    own_cols = pl.ds(pl.multiple_of(tp * cols, cols), cols)

    def local_copies(t):
        copies = [
            (x_hbm.at[0, t], xrow.at[t]),
            (x_hbm.at[0, t, :, own_cols], xh.at[t, own_rows, :]),
            (k_hbm.at[0, t, pl.ds(0, HALF)], kb.at[t, 0]),
            (k_hbm.at[0, t, pl.ds(HALF, HALF)], kb.at[t, high_first]),
            (v_hbm.at[0, t, pl.ds(0, HALF)], vb.at[t, 0]),
            (v_hbm.at[0, t, pl.ds(HALF, HALF)], vb.at[t, high_first]),
        ]
        if t == 0:
            copies.append((w_hbm.at[0, :, own_cols], ah.at[t, own_rows, :]))
        return [
            functools.partial(pltpu.make_async_copy, s, d, local_sem.at[t, i])
            for i, (s, d) in enumerate(copies)
        ]

    def own_output_grad(t):
        return pltpu.make_async_copy(
            og_hbm.at[t - 1, :, own_cols], ah.at[t, own_rows, :], local_sem.at[t, 6]
        )

    for t in range(ticks):
        for c in local_copies(t):
            c().start()
        if t > 0:

            @pl.when(seg == last)
            def _(t=t):
                own_output_grad(t).start()

    odd = lax.rem(me, 2)
    pad_slot = (1 - odd) * (me + 1) + odd * (n + 1)
    for t in range(ticks):
        kb[t, pad_slot] = jnp.zeros((HALF, HD), bf16)
        vb[t, pad_slot] = jnp.zeros((HALF, HD), bf16)

    for t in range(ticks):
        local_copies(t)[0]().wait()
        total = jnp.zeros((rows, HD), f32)
        for c in range(width // HD):
            x = xrow[t, :, c * HD : (c + 1) * HD].astype(f32)
            total = total + x * x
        mean = jnp.sum(total, axis=1, keepdims=True) * (1.0 / width)
        invh[t, own_rows, :] = jnp.broadcast_to(lax.rsqrt(mean + EPS), (rows, HD))

    pl.semaphore_wait(barrier, n - 1 + n_tp - 1 + 2)

    def x_send(t, d):
        to = tp_peer(d)
        there = pl.ds(pl.multiple_of(to * cols, cols), cols)
        return remote(
            x_hbm.at[0, t, :, there], xh.at[t, own_rows, :], x_s.at[t, d], x_r.at[t, d], {"tp": to}
        )

    def a_send(t, d):
        to = tp_peer(d)
        there = pl.ds(pl.multiple_of(to * cols, cols), cols)
        src = w_hbm.at[0, :, there] if t == 0 else og_hbm.at[t - 1, :, there]
        return remote(src, ah.at[t, own_rows, :], a_s.at[t, d], a_r.at[t, d], {"tp": to})

    def inv_send(t, d):
        to = tp_peer(d)
        return remote(
            invh.at[t, own_rows, :],
            invh.at[t, own_rows, :],
            inv_s.at[t, d],
            inv_r.at[t, d],
            {"tp": to},
        )

    def kv_sends(t, d):
        to = ctx_peer(d)
        wrapped = (me + d) // n
        slot = (1 - wrapped) * d + wrapped * (2 * ((to + 2) // 2) + n - d)
        section = pl.ds(pl.multiple_of(wrapped * HALF, HALF), HALF)
        return (
            remote(
                k_hbm.at[0, t, section], kb.at[t, slot], k_s.at[t, d], k_r.at[t, slot], {"ctx": to}
            ),
            remote(
                v_hbm.at[0, t, section], vb.at[t, slot], v_s.at[t, d], v_r.at[t, slot], {"ctx": to}
            ),
        )

    def send_kv(t):
        @pl.loop(1, n)
        def _(d):
            for c in kv_sends(t, d):
                c.start()

    for d in range(1, n_tp):
        inv_send(0, d).start()
        x_send(0, d).start()
        a_send(0, d).start()
    send_kv(0)
    for t in range(1, ticks):
        for d in range(1, n_tp):
            inv_send(t, d).start()
            x_send(t, d).start()

            @pl.when(seg == last)
            def _(t=t, d=d):
                a_send(t, d).start()

        send_kv(t)

    def gain_of(g):
        return gain_ref[pl.ds(tp * group + g, 1), :]

    def half_rows(h):
        return slice(h * HALF, (h + 1) * HALF)

    def head_cols(g):
        return slice(g * HD, (g + 1) * HD)

    def normed_of(t, h, g):
        return xh[t, half_rows(h), head_cols(g)].astype(f32) * invh[t, half_rows(h), :]

    def prepare(t, h):
        for g in range(group):
            at = slice(g * HALF, (g + 1) * HALF)
            qs[h, at, :] = (normed_of(t, h, g) * gain_of(g)).astype(bf16)
            dos[h, at, :] = ah[t, half_rows(h), head_cols(g)]

    def wait_slot(t, slot):
        peer = {"ctx": ctx_peer(1)}
        remote(kb.at[t, slot], kb.at[t, slot], k_s.at[t, 0], k_r.at[t, slot], peer).wait_recv()
        remote(vb.at[t, slot], vb.at[t, slot], v_s.at[t, 0], v_r.at[t, slot], peer).wait_recv()

    def wait_pair(t, p, first, count):
        for i in range(2):
            slot = 2 * p + i

            @pl.when((slot > first) & (slot < first + count))
            def _(slot=slot):
                wait_slot(t, slot)

    def pair_bounds(h):
        return (0, low_pairs) if h == 0 else (low_pairs, pairs)

    def scores(t, h):
        lane = lax.broadcasted_iota(jnp.int32, (1, lanes), 1)
        within = lax.rem(lane, HALF)
        if h == 0:
            query_pos = within + HALF * me
            start = jnp.zeros((1, lanes), jnp.int32)
            closing = jnp.int32(0)
            for k in range(docs):
                length = doc_ref[seg + t, k]
                closing = closing + length
                start = start + jnp.where(closing <= query_pos, length, 0)
            section_of_first = me
            first, count = 0, me + 1
        else:
            query_pos = within + HALF * (2 * n - 1 - me)
            start = jnp.full((1, lanes), HALF * n, jnp.int32)
            section_of_first = 2 * n - 1 - me
            first, count = high_first, n - me
        begin, end = pair_bounds(h)
        row = lax.broadcasted_iota(jnp.int32, (2 * HALF, chunk), 0)
        row = jnp.where(row < HALF, row, row - 2 * HALF)

        @pl.loop(begin, end)
        def _(p):
            wait_pair(t, p, first, count)
            key_pair = kb[t, pl.ds(2 * p, 2)].reshape(2 * HALF, HD)
            value_pair = vb[t, pl.ds(2 * p, 2)].reshape(2 * HALF, HD)
            base = HALF * (section_of_first - (2 * p - first))
            for c in range(lanes // chunk):
                at = slice(c * chunk, (c + 1) * chunk)
                s = dot_nt(key_pair, qs[h, at, :])
                upper = query_pos[:, at] - base
                lower = start[:, at] - base
                s = jnp.where((row <= upper) & (row >= lower), s, MASKED)
                peak = jnp.max(s, axis=0, keepdims=True)
                e = jnp.exp2((s - peak) * EXP2_SCALE)
                dp = dot_nt(value_pair, dos[h, at, :])
                m_ref[p, :, at] = peak
                l_ref[p, :, at] = jnp.sum(e, axis=0, keepdims=True)
                w_ref[p, :, at] = jnp.sum(e * dp, axis=0, keepdims=True)
                e_ref[p, :, at] = e
                dp_ref[p, :, at] = dp

    def combine(h):
        begin, end = pair_bounds(h)
        peak = lax.fori_loop(
            begin,
            end,
            lambda p, m: jnp.maximum(m, m_ref[p]),
            jnp.full((1, lanes), MASKED, f32),
        )

        def add(p, carry):
            total, weighted = carry
            alpha = jnp.exp2((m_ref[p] - peak) * EXP2_SCALE)
            m_ref[p] = alpha
            return total + alpha * l_ref[p], weighted + alpha * w_ref[p]

        zero = jnp.zeros((1, lanes), f32)
        total, weighted = lax.fori_loop(begin, end, add, (zero, zero))
        inverse_total = 1.0 / total
        rt_ref[h] = weighted * inverse_total

        @pl.loop(begin, end)
        def _(p):
            m_ref[p] = m_ref[p] * inverse_total

    def gradients(t, h):
        begin, end = pair_bounds(h)
        dqt[h] = jnp.zeros((HD, lanes), f32)

        @pl.loop(begin, end)
        def _(p):
            key_pair = kb[t, pl.ds(2 * p, 2)].reshape(2 * HALF, HD)
            dk = jnp.zeros((2 * HALF, HD), f32)
            dv = jnp.zeros((2 * HALF, HD), f32)
            for c in range(lanes // chunk):
                at = slice(c * chunk, (c + 1) * chunk)
                probs = e_ref[p, :, at] * m_ref[p, :, at]
                dscore = (probs * (dp_ref[p, :, at] - rt_ref[h, :, at])).astype(bf16)
                dv = dv + jnp.dot(probs.astype(bf16), dos[h, at, :], preferred_element_type=f32)
                dk = dk + jnp.dot(dscore, qs[h, at, :], preferred_element_type=f32)
                dqt[h, :, at] += dot_tn(key_pair, dscore)
            dk = (dk * SCALE).reshape(2, HALF, HD)
            dv = dv.reshape(2, HALF, HD)
            dkf[t, pl.ds(2 * p, 2)] = dk
            dvf[t, pl.ds(2 * p, 2)] = dv
            dks[t, pl.ds(2 * p, 2)] = dk.astype(bf16)
            dvs[t, pl.ds(2 * p, 2)] = dv.astype(bf16)

    def grad_sends(t, d):
        to = ctx_behind(d)
        slot = slot_of(d)
        return (
            remote(dks.at[t, slot], gk.at[t, d], dk_s.at[t, d], dk_r.at[t, d], {"ctx": to}),
            remote(dvs.at[t, slot], gv.at[t, d], dv_s.at[t, d], dv_r.at[t, d], {"ctx": to}),
        )

    def send_grads(t, h):
        begin, end = (1, me + 1) if h == 0 else (me + 1, n)

        @pl.loop(begin, end)
        def _(d):
            for c in grad_sends(t, d):
                c.start()

    def coupling_send(t, h, d):
        return remote(
            cs.at[t, h], cr.at[t, h, d], c_s.at[t, h, d], c_r.at[t, h, d], {"tp": tp_peer(d)}
        )

    def couple(t, h):
        dq = jnp.transpose(dqt[h] * SCALE)
        low = dq.astype(bf16)
        dqs[h] = low
        part = jnp.zeros((HALF, HD), f32)
        for g in range(group):
            rounded = low[g * HALF : (g + 1) * HALF, :].astype(f32)
            product = rounded * normed_of(t, h, g)
            gacc[pl.ds(g, 1), :] += jnp.sum(product, axis=0, keepdims=True)
            part = part + product * gain_of(g)
        part = jnp.sum(part, axis=1, keepdims=True)
        cs[t, h] = jnp.broadcast_to(part, (HALF, HD))
        for d in range(1, n_tp):
            coupling_send(t, h, d).start()

    def pipe_send(t, h):
        there = ah.at[t + 1, half_rows(h), :]
        return remote(
            ig.at[t, half_rows(h), :],
            there,
            p_s.at[t, h],
            p_r.at[t, h],
            {"pipe": lax.rem(seg + n_pipe - 1, n_pipe)},
        )

    def out_send(t, j):
        d = lax.rem(j + n_tp - tp, n_tp)
        return remote(
            ig.at[t, j * rows : (j + 1) * rows, :],
            ig_out.at[0, t, :, own_cols],
            o_s.at[t, d],
            o_r.at[t, d],
            {"tp": j},
        )

    def out_own(t):
        return pltpu.make_async_copy(
            ig.at[t, own_rows, :], ig_out.at[0, t, :, own_cols], o_s.at[t, 0]
        )

    per_half = n_tp // 2

    def finish(t, h):
        total = cs[t, h]
        for d in range(1, n_tp):
            coupling_send(t, h, d).wait_recv()
            total = total + cr[t, h, d]
        coupling = total * (1.0 / width)
        for g in range(group):
            normed = normed_of(t, h, g)
            scaled = dqs[h, g * HALF : (g + 1) * HALF, :].astype(f32) * gain_of(g)
            arriving = ah[t, half_rows(h), head_cols(g)].astype(f32)
            result = arriving + invh[t, half_rows(h), :] * (scaled - normed * coupling)
            ig[t, half_rows(h), head_cols(g)] = result.astype(bf16)
        if t + 1 < ticks:

            @pl.when(seg > 0)
            def _():
                pipe_send(t, h).start()

        for j in range(h * per_half, (h + 1) * per_half):

            @pl.when(tp != j)
            def _(j=j):
                out_send(t, j).start()

            @pl.when(tp == j)
            def _():
                out_own(t).start()

    gacc[...] = jnp.zeros((group, HD), f32)
    for t in range(ticks):
        for c in local_copies(t)[1:]:
            c().wait()
        for d in range(1, n_tp):
            inv_send(t, d).wait_recv()
            x_send(t, d).wait_recv()
        if t == 0:
            for d in range(1, n_tp):
                a_send(t, d).wait_recv()
        else:

            @pl.when(seg == last)
            def _(t=t):
                own_output_grad(t).wait()
                for d in range(1, n_tp):
                    a_send(t, d).wait_recv()

        for h in range(2):
            if t > 0:

                @pl.when(seg < last)
                def _(t=t, h=h):
                    pipe_send(t - 1, h).wait_recv()

            prepare(t, h)
            scores(t, h)
        for h in range(2):
            combine(h)
            gradients(t, h)
            send_grads(t, h)
            couple(t, h)
        for h in range(2):
            finish(t, h)

    def gain_send(d):
        return remote(gacc, gr.at[d], g_s.at[d], g_r.at[d], {"ctx": ctx_peer(d)})

    @pl.loop(1, n)
    def _(d):
        gain_send(d).start()

    def result_copies(t):
        return (
            pltpu.make_async_copy(dko.at[t], dk_out.at[0, t], local_sem.at[t, 7]),
            pltpu.make_async_copy(dvo.at[t], dv_out.at[0, t], local_sem.at[t, 8]),
        )

    for t in range(ticks):
        for i, (mine, at) in enumerate(((0, slice(0, HALF)), (high_first, slice(HALF, 2 * HALF)))):
            begin, end = (1, n - me) if i == 0 else (n - me, n)

            def add(d, carry, t=t):
                for c in grad_sends(t, d):
                    c.wait_recv()
                return (carry[0] + gk[t, d].astype(f32), carry[1] + gv[t, d].astype(f32))

            dk, dv = lax.fori_loop(begin, end, add, (dkf[t, mine], dvf[t, mine]))
            dko[t, at, :] = dk
            dvo[t, at, :] = dv
        for c in result_copies(t):
            c.start()

    def add_gain(d, total):
        gain_send(d).wait_recv()
        return total + gr[d]

    gain_total = lax.fori_loop(1, n, add_gain, gacc[...])
    gr[0] = gain_total
    own_gain = pl.ds(pl.multiple_of(tp * group, group), group)

    def gain_share(d):
        return remote(
            gr.at[0], gain_out.at[own_gain, :], h_s.at[d], h_r.at[d], {"tp": tp_peer(d)}
        )

    own_gain_copy = pltpu.make_async_copy(gr.at[0], gain_out.at[own_gain, :], h_s.at[0])
    own_gain_copy.start()
    for d in range(1, n_tp):
        gain_share(d).start()

    for t in range(ticks):
        for d in range(1, n_tp):
            inv_send(t, d).wait_send()
            x_send(t, d).wait_send()
            if t == 0:
                a_send(t, d).wait_send()
            else:

                @pl.when(seg == last)
                def _(t=t, d=d):
                    a_send(t, d).wait_send()

            for h in range(2):
                coupling_send(t, h, d).wait_send()

        @pl.loop(1, n)
        def _(d, t=t):
            for c in kv_sends(t, d):
                c.wait_send()
            for c in grad_sends(t, d):
                c.wait_send()

        if t + 1 < ticks:
            for h in range(2):

                @pl.when(seg > 0)
                def _(t=t, h=h):
                    pipe_send(t, h).wait_send()

        for j in range(n_tp):

            @pl.when(tp != j)
            def _(t=t, j=j):
                out_send(t, j).wait_send()

            @pl.when(tp == j)
            def _(t=t):
                out_own(t).wait()

        for d in range(1, n_tp):
            came = ig_out.at[0, t, :, own_cols]
            remote(came, came, o_s.at[t, d], o_r.at[t, d], {"tp": tp_peer(d)}).wait_recv()
        for c in result_copies(t):
            c.wait()

    @pl.loop(1, n)
    def _(d):
        gain_send(d).wait_send()

    own_gain_copy.wait()
    for d in range(1, n_tp):
        gain_share(d).wait_send()
        gain_share(d).wait_recv()


def solution(mesh):
    n_pipe, n_ctx, n_tp = (mesh.shape[a] for a in ("pipe", "ctx", "tp"))

    def on_device(segment_inputs, keys, values, norm_gain, waiting_grads, output_grads, doc_lengths):
        ticks, rows, width = segment_inputs.shape[1:]
        cols = width // n_tp
        group = cols // HD
        docs = doc_lengths.shape[1]
        lanes = group * HALF
        slots = n_ctx + 2
        pairs = slots // 2
        dims = (n_pipe, n_ctx, n_tp, ticks, group, docs)
        dma = pltpu.SemaphoreType.DMA
        vmem = pltpu.VMEM
        hbm = pl.BlockSpec(memory_space=pl.ANY)
        scratch = [
            vmem((ticks, rows, width), bf16),
            vmem((ticks, 2 * HALF, cols), bf16),
            vmem((ticks, 2 * HALF, cols), bf16),
            vmem((ticks, 2 * HALF, HD), f32),
            vmem((ticks, slots, HALF, HD), bf16),
            vmem((ticks, slots, HALF, HD), bf16),
            vmem((2, lanes, HD), bf16),
            vmem((2, lanes, HD), bf16),
            vmem((pairs, 2 * HALF, lanes), f32),
            vmem((pairs, 2 * HALF, lanes), f32),
            vmem((pairs, 1, lanes), f32),
            vmem((pairs, 1, lanes), f32),
            vmem((pairs, 1, lanes), f32),
            vmem((2, 1, lanes), f32),
            vmem((2, HD, lanes), f32),
            vmem((2, lanes, HD), bf16),
            vmem((ticks, slots, HALF, HD), f32),
            vmem((ticks, slots, HALF, HD), f32),
            vmem((ticks, slots, HALF, HD), bf16),
            vmem((ticks, slots, HALF, HD), bf16),
            vmem((ticks, n_ctx, HALF, HD), bf16),
            vmem((ticks, n_ctx, HALF, HD), bf16),
            vmem((ticks, 2 * HALF, cols), bf16),
            vmem((ticks, 2, HALF, HD), f32),
            vmem((ticks, 2, n_tp, HALF, HD), f32),
            vmem((group, HD), f32),
            vmem((n_ctx, group, HD), f32),
            vmem((ticks, 2 * HALF, HD), f32),
            vmem((ticks, 2 * HALF, HD), f32),
            dma((ticks, 9)),
            dma((ticks, n_tp)),
            dma((ticks, n_tp)),
            dma((ticks, n_tp)),
            dma((ticks, n_tp)),
            dma((ticks, n_tp)),
            dma((ticks, n_tp)),
            dma((ticks, n_ctx)),
            dma((ticks, slots)),
            dma((ticks, n_ctx)),
            dma((ticks, slots)),
            dma((ticks, n_ctx)),
            dma((ticks, n_ctx)),
            dma((ticks, n_ctx)),
            dma((ticks, n_ctx)),
            dma((ticks, 2, n_tp)),
            dma((ticks, 2, n_tp)),
            dma((ticks, 2)),
            dma((ticks, 2)),
            dma((ticks, n_tp)),
            dma((ticks, n_tp)),
            dma((n_ctx,)),
            dma((n_ctx,)),
            dma((n_tp,)),
            dma((n_tp,)),
        ]
        input_grads, key_grads, value_grads, gain_grads = pl.pallas_call(
            functools.partial(kernel, dims),
            out_shape=(
                jax.ShapeDtypeStruct((1, ticks, rows, width), bf16),
                jax.ShapeDtypeStruct((1, ticks, 2 * HALF, HD), f32),
                jax.ShapeDtypeStruct((1, ticks, 2 * HALF, HD), f32),
                jax.ShapeDtypeStruct((width // HD, HD), f32),
            ),
            in_specs=[
                hbm,
                hbm,
                hbm,
                pl.BlockSpec(memory_space=pltpu.VMEM),
                hbm,
                hbm,
                pl.BlockSpec(memory_space=pltpu.SMEM),
            ],
            out_specs=(hbm, hbm, hbm, hbm),
            scratch_shapes=scratch,
            compiler_params=pltpu.CompilerParams(
                collective_id=0, has_side_effects=True, vmem_limit_bytes=48 << 20
            ),
            name="window",
        )(
            segment_inputs,
            keys,
            values,
            norm_gain.reshape(width // HD, HD),
            waiting_grads,
            output_grads,
            doc_lengths,
        )
        return input_grads, key_grads, value_grads, gain_grads.reshape(1, width)

    in_specs = (
        P("pipe", None, ("ctx", "tp"), None),
        P("pipe", None, "ctx", "tp"),
        P("pipe", None, "ctx", "tp"),
        P("pipe", None),
        P("pipe", ("ctx", "tp"), None),
        P(None, ("ctx", "tp"), None),
        P(),
    )
    out_specs = (
        P("pipe", None, ("ctx", "tp"), None),
        P("pipe", None, "ctx", "tp"),
        P("pipe", None, "ctx", "tp"),
        P("pipe", None),
    )
    return jax.shard_map(
        on_device, mesh=mesh, in_specs=in_specs, out_specs=out_specs, check_vma=False
    )
```

```python
import functools
import math

import jax
import jax.numpy as jnp
from jax import lax
from jax.experimental import pallas as pl
from jax.experimental.pallas import tpu as pltpu
from jax.sharding import PartitionSpec as P

HD = 128
HALF = 64
EPS = 1e-05
MASKED = -1e30
SCALE = HD ** (-0.5)
EXP2_SCALE = SCALE * math.log2(math.e)
KERNEL_VMEM = 60 << 20
MESH = pl.DeviceIdType.MESH
f32 = jnp.float32
bf16 = jnp.bfloat16


def remote(src, dst, send_sem, recv_sem, device):
    return pltpu.make_async_remote_copy(
        src_ref=src,
        dst_ref=dst,
        send_sem=send_sem,
        recv_sem=recv_sem,
        device_id=device,
        device_id_type=MESH,
    )


def dot_nt(a, b):
    return lax.dot_general(a, b, (((1,), (1,)), ((), ())), preferred_element_type=f32)


def dot_tn(a, b):
    return lax.dot_general(a, b, (((0,), (0,)), ((), ())), preferred_element_type=f32)


def kernel(
    dims,
    x_hbm,
    k_hbm,
    v_hbm,
    gain_ref,
    w_hbm,
    og_hbm,
    doc_ref,
    ig_out,
    dk_out,
    dv_out,
    gain_out,
    xrow,
    xh,
    ah,
    invh,
    kv,
    qs,
    dos,
    e_ref,
    dp_ref,
    m_ref,
    l_ref,
    rt_ref,
    dqt,
    dqs,
    gf,
    gb,
    gp,
    gs,
    gz,
    ig,
    cs,
    cr,
    gacc,
    gr,
    res,
    local_sem,
    x_s,
    x_r,
    a_s,
    a_r,
    inv_s,
    inv_r,
    kv_s,
    kv_r,
    fw_s,
    gp_s,
    gp_r,
    gz_s,
    gz_r,
    c_s,
    c_r,
    p_s,
    p_r,
    o_s,
    o_r,
    g_s,
    g_r,
    h_s,
    h_r,
):
    n_pipe, n_ctx, n_tp, ticks, group, docs = dims
    n = n_ctx
    rows = 2 * HALF // n_tp
    cols = group * HD
    width = n_tp * cols
    lanes = group * HALF
    chunk = 256
    pairs = (n + 2) // 2

    seg = lax.axis_index("pipe")
    me = lax.axis_index("ctx")
    tp = lax.axis_index("tp")
    last = n_pipe - 1
    low_pairs = (me + 2) // 2
    high_first = 2 * low_pairs

    def ctx_peer(d):
        return lax.rem(me + d, n)

    def ctx_behind(d):
        return lax.rem(me + n - d, n)

    def tp_peer(d):
        return lax.rem(tp + d, n_tp)

    line = lax.rem(me, 2)
    partner = me + 1 - 2 * line
    lines = n // 2
    far_first = sorted(range(1, lines), key=lambda i: -min(i, lines - i))

    def upper(d):
        return (n + d - 1 - me) // n

    def slot_of(d):
        return (1 - upper(d)) * d + upper(d) * (high_first + n - d)

    def partner_slot(slot, is_upper):
        return slot + (1 - 2 * line) * (1 - 2 * is_upper)

    barrier = pltpu.get_barrier_semaphore()

    @pl.loop(1, n)
    def _(d):
        pl.semaphore_signal(barrier, inc=1, device_id={"ctx": ctx_peer(d)}, device_id_type=MESH)

    for d in range(1, n_tp):
        pl.semaphore_signal(barrier, inc=1, device_id={"tp": tp_peer(d)}, device_id_type=MESH)
    pl.semaphore_signal(
        barrier, inc=1, device_id={"pipe": lax.rem(seg + 1, n_pipe)}, device_id_type=MESH
    )
    pl.semaphore_signal(
        barrier, inc=1, device_id={"pipe": lax.rem(seg + n_pipe - 1, n_pipe)}, device_id_type=MESH
    )

    own_rows = pl.ds(pl.multiple_of(tp * rows, rows), rows)
    own_cols = pl.ds(pl.multiple_of(tp * cols, cols), cols)

    def kv_copies(t):
        return [
            pltpu.make_async_copy(
                ref.at[0, t, pl.ds(i * HALF, HALF)], kv.at[t, slot, which], local_sem.at[t, 2 * which + i]
            )
            for which, ref in enumerate((k_hbm, v_hbm))
            for i, slot in enumerate((0, high_first))
        ]

    def x_copy(t):
        return pltpu.make_async_copy(x_hbm.at[0, t], xrow.at[t], local_sem.at[t, 4])

    def own_x(t):
        return pltpu.make_async_copy(
            x_hbm.at[0, t, :, own_cols], xh.at[t, own_rows, :], local_sem.at[t, 5]
        )

    def own_a(t):
        return pltpu.make_async_copy(
            w_hbm.at[0, :, own_cols], ah.at[t, own_rows, :], local_sem.at[t, 6]
        )

    def own_output_grad(t):
        return pltpu.make_async_copy(
            og_hbm.at[t - 1, :, own_cols], ah.at[t, own_rows, :], local_sem.at[t, 6]
        )

    for t in range(ticks):
        for c in kv_copies(t):
            c.start()
    for t in range(ticks):
        x_copy(t).start()
        own_x(t).start()
        if t == 0:
            own_a(t).start()
        else:

            @pl.when(seg == last)
            def _(t=t):
                own_output_grad(t).start()

    odd = lax.rem(me, 2)
    pad_slot = (1 - odd) * (me + 1) + odd * (n + 1)
    for t in range(ticks):
        kv[t, pad_slot] = jnp.zeros((2, HALF, HD), bf16)
    for t in range(ticks):
        for c in kv_copies(t):
            c.wait()

    pl.semaphore_wait(barrier, n - 1 + n_tp - 1 + 2)

    def x_send(t, d):
        to = tp_peer(d)
        there = pl.ds(pl.multiple_of(to * cols, cols), cols)
        return remote(
            x_hbm.at[0, t, :, there], xh.at[t, own_rows, :], x_s.at[t, d], x_r.at[t, d], {"tp": to}
        )

    def a_send(t, d):
        to = tp_peer(d)
        there = pl.ds(pl.multiple_of(to * cols, cols), cols)
        src = w_hbm.at[0, :, there] if t == 0 else og_hbm.at[t - 1, :, there]
        return remote(src, ah.at[t, own_rows, :], a_s.at[t, d], a_r.at[t, d], {"tp": to})

    def inv_send(t, d):
        to = tp_peer(d)
        return remote(
            invh.at[t, own_rows, :],
            invh.at[t, own_rows, :],
            inv_s.at[t, d],
            inv_r.at[t, d],
            {"tp": to},
        )

    def kv_send(t, which, i):
        d = 2 * i
        to = ctx_peer(d)
        wrapped = (me + d) // n
        slot = (1 - wrapped) * d + wrapped * (2 * ((to + 2) // 2) + n - d)
        return remote(
            kv.at[t, wrapped * high_first, which],
            kv.at[t, slot, which],
            kv_s.at[t, which, i],
            kv_r.at[t, which, slot],
            {"ctx": to},
        )

    def kv_forward(t, which, i):
        if i == 0:
            slot, is_upper = line * high_first, line
        else:
            slot, is_upper = slot_of(2 * i), upper(2 * i)
        there = partner_slot(slot, is_upper)
        return remote(
            kv.at[t, slot, which],
            kv.at[t, there, which],
            fw_s.at[t, which, i],
            kv_r.at[t, which, there],
            {"ctx": partner},
        )

    def kv_wait(t, which, slot):
        came = kv.at[t, slot, which]
        remote(
            came, came, kv_s.at[t, which, 0], kv_r.at[t, which, slot], {"ctx": partner}
        ).wait_recv()

    def send_kv(t, which):
        kv_forward(t, which, 0).start()
        for i in far_first:
            kv_send(t, which, i).start()

    def forward_kv(t, which):
        for i in far_first:
            kv_wait(t, which, slot_of(2 * i))
            kv_forward(t, which, i).start()

    def inverse(t):
        x_copy(t).wait()
        total = jnp.zeros((rows, HD), f32)
        for c in range(width // HD):
            x = xrow[t, :, c * HD : (c + 1) * HD].astype(f32)
            total = total + x * x
        mean = jnp.sum(total, axis=1, keepdims=True) * (1.0 / width)
        invh[t, own_rows, :] = jnp.broadcast_to(lax.rsqrt(mean + EPS), (rows, HD))
        for d in range(1, n_tp):
            inv_send(t, d).start()

    for t in range(ticks):
        for which in range(2):
            send_kv(t, which)
        inverse(t)
        for d in range(1, n_tp):
            x_send(t, d).start()
        for d in range(1, n_tp):
            if t == 0:
                a_send(t, d).start()
            else:

                @pl.when(seg == last)
                def _(t=t, d=d):
                    a_send(t, d).start()

    def gain_of(g):
        return gain_ref[pl.ds(tp * group + g, 1), :]

    def half_rows(h):
        return slice(h * HALF, (h + 1) * HALF)

    def head_cols(g):
        return slice(g * HD, (g + 1) * HD)

    def normed_of(t, h, g):
        return xh[t, half_rows(h), head_cols(g)].astype(f32) * invh[t, half_rows(h), :]

    def head_rows(g):
        return slice(g * HALF, (g + 1) * HALF)

    def prepare_queries(t, h):
        for g in range(group):
            qs[t, h, head_rows(g), :] = (normed_of(t, h, g) * gain_of(g)).astype(bf16)

    def prepare_arriving(t, h):
        for g in range(group):
            dos[h, head_rows(g), :] = ah[t, half_rows(h), head_cols(g)]

    unroll = 3 if pairs % 3 == 0 else 1

    def each_group(step):
        @pl.loop(0, pairs // unroll)
        def _(i):
            step([i * unroll + u for u in range(unroll)])

    def half_of(p):
        return (p - low_pairs + n) // n

    def pair_of(t, p, which):
        return kv[t, pl.ds(2 * p, 2), which].reshape(2 * HALF, HD)

    chunks = [slice(c * chunk, (c + 1) * chunk) for c in range(lanes // chunk)]

    def wait_forwarded(t, which, p):
        h = half_of(p)

        @pl.when(2 * p + 1 < (1 - h) * (me + 1) + h * (high_first + n - me))
        def _():
            kv_wait(t, which, 2 * p + 1)

    def by_half(values, combine, empty):
        result = [jnp.full((1, lanes), empty, f32) for _ in range(2)]
        for p, value in enumerate(values):
            is_low = p < low_pairs
            result[0] = combine(result[0], jnp.where(is_low, value, empty))
            result[1] = combine(result[1], jnp.where(is_low, empty, value))
        return result

    def softmax(t):
        within = lax.rem(lax.broadcasted_iota(jnp.int32, (1, lanes), 1), HALF)
        low_pos = within + HALF * me
        low_start = jnp.zeros((1, lanes), jnp.int32)
        closing = jnp.int32(0)
        for k in range(docs):
            length = doc_ref[seg + t, k]
            closing = closing + length
            low_start = low_start + jnp.where(closing <= low_pos, length, 0)
        row = lax.broadcasted_iota(jnp.int32, (2 * HALF, chunk), 0)
        row = jnp.where(row < HALF, row, row - 2 * HALF)

        def step(group_pairs):
            for p in group_pairs:
                wait_forwarded(t, 0, p)
            for p in group_pairs:
                h = half_of(p)
                section = (1 - h) * me + h * (2 * n - 1 - me)
                base = HALF * (section - (2 * p - h * high_first))
                up_to = within + (HALF * section - base)
                down_to = jnp.where(h == 0, low_start, HALF * n) - base
                key_pair = pair_of(t, p, 0)
                for at in chunks:
                    s = dot_nt(key_pair, qs[t, h, at, :])
                    s = jnp.where((row <= up_to[:, at]) & (row >= down_to[:, at]), s, MASKED)
                    peak = jnp.max(s, axis=0, keepdims=True)
                    e = jnp.exp2((s - peak) * EXP2_SCALE)
                    m_ref[t, p, :, at] = peak
                    l_ref[p, :, at] = jnp.sum(e, axis=0, keepdims=True)
                    e_ref[t, p, :, at] = e

        each_group(step)
        peaks = [m_ref[t, p] for p in range(pairs)]
        peak = by_half(peaks, jnp.maximum, MASKED)
        alphas = [
            jnp.exp2((m - jnp.where(p < low_pairs, peak[0], peak[1])) * EXP2_SCALE)
            for p, m in enumerate(peaks)
        ]
        total = by_half([a * l_ref[p] for p, a in enumerate(alphas)], jnp.add, 0.0)
        inverse_total = [1.0 / part for part in total]
        for p, alpha in enumerate(alphas):
            m_ref[t, p] = alpha * jnp.where(p < low_pairs, inverse_total[0], inverse_total[1])

    def put_gradient(t, p, which, value):
        value = value.reshape(2, HALF, HD)
        gf[t, pl.ds(2 * p, 2), which] = value
        gb[t, pl.ds(2 * p, 2), which] = value.astype(bf16)

    def values_pass(t):
        def step(group_pairs):
            for p in group_pairs:
                wait_forwarded(t, 1, p)
            for p in group_pairs:
                h = half_of(p)
                value_pair = pair_of(t, p, 1)
                dv = jnp.zeros((2 * HALF, HD), f32)
                for at in chunks:
                    grads = dos[h, at, :]
                    probs = e_ref[t, p, :, at] * m_ref[t, p, :, at]
                    dp = dot_nt(value_pair, grads)
                    dv = dv + jnp.dot(probs.astype(bf16), grads, preferred_element_type=f32)
                    l_ref[p, :, at] = jnp.sum(probs * dp, axis=0, keepdims=True)
                    dp_ref[p, :, at] = dp
                put_gradient(t, p, 1, dv)

        each_group(step)
        terms = by_half([l_ref[p] for p in range(pairs)], jnp.add, 0.0)
        for h in range(2):
            rt_ref[h] = terms[h]

    def keys_pass(t):
        for h in range(2):
            dqt[h] = jnp.zeros((HD, lanes), f32)

        def step(group_pairs):
            for p in group_pairs:
                h = half_of(p)
                key_pair = pair_of(t, p, 0)
                dk = jnp.zeros((2 * HALF, HD), f32)
                for at in chunks:
                    probs = e_ref[t, p, :, at] * m_ref[t, p, :, at]
                    dscore = (probs * (dp_ref[p, :, at] - rt_ref[h, :, at])).astype(bf16)
                    dk = dk + jnp.dot(dscore, qs[t, h, at, :], preferred_element_type=f32)
                    dqt[h, :, at] += dot_tn(key_pair, dscore)
                put_gradient(t, p, 0, dk * SCALE)

        each_group(step)

    def partner_send(t, which, i):
        d = 2 * i + 1
        slot = slot_of(d)
        there = partner_slot(slot, upper(d))
        return remote(
            gb.at[t, slot, which],
            gp.at[t, there, which],
            gp_s.at[t, which, i],
            gp_r.at[t, which, there],
            {"ctx": partner},
        )

    def send_to_partner(t, which):
        @pl.loop(0, lines)
        def _(i):
            partner_send(t, which, i).start()

    def partner_wait(t, which, slot):
        came = gp.at[t, slot, which]
        remote(
            came, came, gp_s.at[t, which, 0], gp_r.at[t, which, slot], {"ctx": partner}
        ).wait_recv()

    def owner_send(t, which, i):
        return remote(
            gs.at[t, i, which],
            gz.at[t, i, which],
            gz_s.at[t, which, i],
            gz_r.at[t, which, i],
            {"ctx": ctx_behind(2 * i)},
        )

    def send_to_owners(t, which):
        for i in far_first:
            slot = slot_of(2 * i)
            partner_wait(t, which, slot)
            both = gf[t, slot, which] + gp[t, slot, which].astype(f32)
            gs[t, i, which] = both.astype(bf16)
            owner_send(t, which, i).start()

    def coupling_send(t, h, d):
        return remote(
            cs.at[t, h], cr.at[t, h, d], c_s.at[t, h, d], c_r.at[t, h, d], {"tp": tp_peer(d)}
        )

    diagonal = lax.broadcasted_iota(jnp.int32, (HALF, HD), 0) == lax.broadcasted_iota(
        jnp.int32, (HALF, HD), 1
    )

    def couple(t, h):
        dq = jnp.transpose(dqt[h] * SCALE)
        low = dq.astype(bf16)
        dqs[h] = low
        part = jnp.zeros((HALF, HD), f32)
        for g in range(group):
            rounded = low[g * HALF : (g + 1) * HALF, :].astype(f32)
            product = rounded * normed_of(t, h, g)
            gacc[pl.ds(g, 1), :] += jnp.sum(product, axis=0, keepdims=True)
            part = part + product * gain_of(g)
        part = jnp.sum(part, axis=1, keepdims=True)
        cs[t, h] = jnp.sum(jnp.where(diagonal, part, 0.0), axis=0, keepdims=True)
        for d in range(1, n_tp):
            coupling_send(t, h, d).start()

    def pipe_send(t, h):
        there = ah.at[t + 1, half_rows(h), :]
        return remote(
            ig.at[t, half_rows(h), :],
            there,
            p_s.at[t, h],
            p_r.at[t, h],
            {"pipe": lax.rem(seg + n_pipe - 1, n_pipe)},
        )

    def out_send(t, j):
        d = lax.rem(j + n_tp - tp, n_tp)
        return remote(
            ig.at[t, j * rows : (j + 1) * rows, :],
            ig_out.at[0, t, :, own_cols],
            o_s.at[t, d],
            o_r.at[t, d],
            {"tp": j},
        )

    def out_own(t):
        return pltpu.make_async_copy(
            ig.at[t, own_rows, :], ig_out.at[0, t, :, own_cols], o_s.at[t, 0]
        )

    per_half = n_tp // 2

    def finish(t, h):
        total = cs[t, h]
        for d in range(1, n_tp):
            coupling_send(t, h, d).wait_recv()
            total = total + cr[t, h, d]
        coupling = jnp.sum(jnp.where(diagonal, total, 0.0), axis=1, keepdims=True) * (1.0 / width)
        for g in range(group):
            normed = normed_of(t, h, g)
            scaled = dqs[h, g * HALF : (g + 1) * HALF, :].astype(f32) * gain_of(g)
            arriving = ah[t, half_rows(h), head_cols(g)].astype(f32)
            result = arriving + invh[t, half_rows(h), :] * (scaled - normed * coupling)
            ig[t, half_rows(h), head_cols(g)] = result.astype(bf16)
        if t + 1 < ticks:

            @pl.when(seg > 0)
            def _():
                pipe_send(t, h).start()

        for j in range(h * per_half, (h + 1) * per_half):

            @pl.when(tp != j)
            def _(j=j):
                out_send(t, j).start()

            @pl.when(tp == j)
            def _():
                out_own(t).start()

    gacc[...] = jnp.zeros((group, HD), f32)

    def wait_rows(t):
        own_x(t).wait()
        for d in range(1, n_tp):
            inv_send(t, d).wait_recv()
            x_send(t, d).wait_recv()

    def wait_arriving(t, h):
        if t == 0:
            if h == 0:
                own_a(t).wait()
                for d in range(1, n_tp):
                    a_send(t, d).wait_recv()
            return

        @pl.when(seg < last)
        def _():
            pipe_send(t - 1, h).wait_recv()

        if h == 0:

            @pl.when(seg == last)
            def _():
                own_output_grad(t).wait()
                for d in range(1, n_tp):
                    a_send(t, d).wait_recv()

    def queries(t):
        wait_rows(t)
        for h in range(2):
            prepare_queries(t, h)

    def values(t):
        for h in range(2):
            wait_arriving(t, h)
            prepare_arriving(t, h)
        values_pass(t)

    def gain_send(d):
        return remote(gacc, gr.at[d], g_s.at[d], g_r.at[d], {"ctx": ctx_peer(d)})

    def add_gain(d, total):
        gain_send(d).wait_recv()
        return total + gr[d]

    own_gain = pl.ds(pl.multiple_of(tp * group, group), group)

    def gain_share(d):
        return remote(
            gr.at[0], gain_out.at[own_gain, :], h_s.at[d], h_r.at[d], {"tp": tp_peer(d)}
        )

    for which in range(2):
        forward_kv(0, which)
    queries(0)
    softmax(0)
    for which in range(2):
        forward_kv(1, which)
    values(0)
    keys_pass(0)
    for h in range(2):
        couple(0, h)
    queries(1)
    for h in range(2):
        finish(0, h)
    for which in range(2):
        send_to_partner(0, which)
    softmax(1)
    values(1)
    send_to_partner(1, 1)
    for which in range(2):
        send_to_owners(0, which)
    keys_pass(1)
    send_to_partner(1, 0)
    for h in range(2):
        couple(1, h)

    @pl.loop(1, n)
    def _(d):
        gain_send(d).start()

    send_to_owners(1, 1)
    for h in range(2):
        finish(1, h)
    send_to_owners(1, 0)
    gain_total = lax.fori_loop(1, n, add_gain, gacc[...])
    gr[0] = gain_total
    own_gain_copy = pltpu.make_async_copy(gr.at[0], gain_out.at[own_gain, :], h_s.at[0])
    own_gain_copy.start()
    for d in range(1, n_tp):
        gain_share(d).start()

    def result_copy(t, which):
        out = (dk_out, dv_out)[which]
        return pltpu.make_async_copy(res.at[t, which], out.at[0, t], local_sem.at[t, which])

    for t in range(ticks):
        for which in (1, 0):
            partner_wait(t, which, line * high_first)
            for i, mine in enumerate((0, high_first)):
                middle = (n + 1 - me) // 2
                begin, end = (1, middle) if i == 0 else (middle, lines)
                from_partner = jnp.where(line == i, gp[t, mine, which].astype(f32), 0.0)

                def add(k, total, t=t, which=which):
                    owner_send(t, which, k).wait_recv()
                    return total + gz[t, k, which].astype(f32)

                res[t, which, half_rows(i), :] = lax.fori_loop(
                    begin, end, add, gf[t, mine, which] + from_partner
                )
            result_copy(t, which).start()

    for t in range(ticks):
        for d in range(1, n_tp):
            inv_send(t, d).wait_send()
            x_send(t, d).wait_send()
            if t == 0:
                a_send(t, d).wait_send()
            else:

                @pl.when(seg == last)
                def _(t=t, d=d):
                    a_send(t, d).wait_send()

            for h in range(2):
                coupling_send(t, h, d).wait_send()

        for which in range(2):
            for i in range(lines):
                kv_forward(t, which, i).wait_send()
                if i > 0:
                    kv_send(t, which, i).wait_send()
                    owner_send(t, which, i).wait_send()

            @pl.loop(0, lines)
            def _(i, t=t, which=which):
                partner_send(t, which, i).wait_send()

            result_copy(t, which).wait()

        if t + 1 < ticks:
            for h in range(2):

                @pl.when(seg > 0)
                def _(t=t, h=h):
                    pipe_send(t, h).wait_send()

        for j in range(n_tp):

            @pl.when(tp != j)
            def _(t=t, j=j):
                out_send(t, j).wait_send()

            @pl.when(tp == j)
            def _(t=t):
                out_own(t).wait()

        for d in range(1, n_tp):
            came = ig_out.at[0, t, :, own_cols]
            remote(came, came, o_s.at[t, d], o_r.at[t, d], {"tp": tp_peer(d)}).wait_recv()
    @pl.loop(1, n)
    def _(d):
        gain_send(d).wait_send()

    own_gain_copy.wait()

    for d in range(1, n_tp):
        gain_share(d).wait_send()
        gain_share(d).wait_recv()


def hand_over(*refs):
    *refs, sems = refs
    count = len(refs) // 3
    came, left, held = refs[:count], refs[count : 2 * count], refs[2 * count :]
    loads = [pltpu.make_async_copy(came[i], held[i], sems.at[0, i]) for i in range(count)]
    stores = [pltpu.make_async_copy(held[i], left[i], sems.at[1, i]) for i in range(count)]
    for c in loads:
        c.start()
    for load, store in zip(loads, stores):
        load.wait()
        store.start()
    for c in stores:
        c.wait()


def solution(mesh):
    n_pipe, n_ctx, n_tp = (mesh.shape[a] for a in ("pipe", "ctx", "tp"))

    def on_device(segment_inputs, keys, values, norm_gain, waiting_grads, output_grads, doc_lengths):
        ticks, rows, width = segment_inputs.shape[1:]
        cols = width // n_tp
        group = cols // HD
        docs = doc_lengths.shape[1]
        lanes = group * HALF
        slots = n_ctx + 2
        pairs = slots // 2
        dims = (n_pipe, n_ctx, n_tp, ticks, group, docs)
        dma = pltpu.SemaphoreType.DMA
        vmem = pltpu.VMEM
        hbm = pl.BlockSpec(memory_space=pl.ANY)
        lines = n_ctx // 2
        scratch = [
            vmem((ticks, rows, width), bf16),
            vmem((ticks, 2 * HALF, cols), bf16),
            vmem((ticks, 2 * HALF, cols), bf16),
            vmem((ticks, 2 * HALF, HD), f32),
            vmem((ticks, slots, 2, HALF, HD), bf16),
            vmem((ticks, 2, lanes, HD), bf16),
            vmem((2, lanes, HD), bf16),
            vmem((ticks, pairs, 2 * HALF, lanes), f32),
            vmem((pairs, 2 * HALF, lanes), f32),
            vmem((ticks, pairs, 1, lanes), f32),
            vmem((pairs, 1, lanes), f32),
            vmem((2, 1, lanes), f32),
            vmem((2, HD, lanes), f32),
            vmem((2, lanes, HD), bf16),
            vmem((ticks, slots, 2, HALF, HD), f32),
            vmem((ticks, slots, 2, HALF, HD), bf16),
            vmem((ticks, slots, 2, HALF, HD), bf16),
            vmem((ticks, lines, 2, HALF, HD), bf16),
            vmem((ticks, lines, 2, HALF, HD), bf16),
            vmem((ticks, 2 * HALF, cols), bf16),
            vmem((ticks, 2, 1, HD), f32),
            vmem((ticks, 2, n_tp, 1, HD), f32),
            vmem((group, HD), f32),
            vmem((n_ctx, group, HD), f32),
            vmem((ticks, 2, 2 * HALF, HD), f32),
            dma((ticks, 7)),
            dma((ticks, n_tp)),
            dma((ticks, n_tp)),
            dma((ticks, n_tp)),
            dma((ticks, n_tp)),
            dma((ticks, n_tp)),
            dma((ticks, n_tp)),
            dma((ticks, 2, lines)),
            dma((ticks, 2, slots)),
            dma((ticks, 2, lines)),
            dma((ticks, 2, lines)),
            dma((ticks, 2, slots)),
            dma((ticks, 2, lines)),
            dma((ticks, 2, lines)),
            dma((ticks, 2, n_tp)),
            dma((ticks, 2, n_tp)),
            dma((ticks, 2)),
            dma((ticks, 2)),
            dma((ticks, n_tp)),
            dma((ticks, n_tp)),
            dma((n_ctx,)),
            dma((n_ctx,)),
            dma((n_tp,)),
            dma((n_tp,)),
        ]
        on_chip = pl.BlockSpec(memory_space=pltpu.VMEM)
        input_grads, key_grads, value_grads, gain_grads = pl.pallas_call(
            functools.partial(kernel, dims),
            out_shape=(
                jax.ShapeDtypeStruct((1, ticks, rows, width), bf16),
                jax.ShapeDtypeStruct((1, ticks, 2 * HALF, HD), f32),
                jax.ShapeDtypeStruct((1, ticks, 2 * HALF, HD), f32),
                jax.ShapeDtypeStruct((width // HD, HD), f32),
            ),
            in_specs=[
                hbm,
                hbm,
                hbm,
                on_chip,
                hbm,
                hbm,
                pl.BlockSpec(memory_space=pltpu.SMEM),
            ],
            out_specs=(hbm,) * 4,
            scratch_shapes=scratch,
            compiler_params=pltpu.CompilerParams(
                collective_id=0, has_side_effects=True, vmem_limit_bytes=KERNEL_VMEM
            ),
            name="window",
        )(
            segment_inputs,
            keys,
            values,
            norm_gain.reshape(width // HD, HD),
            waiting_grads,
            output_grads,
            doc_lengths,
        )
        made = (input_grads, key_grads, value_grads, gain_grads)
        input_grads, key_grads, value_grads, gain_grads = pl.pallas_call(
            hand_over,
            out_shape=tuple(jax.ShapeDtypeStruct(a.shape, a.dtype) for a in made),
            in_specs=[hbm] * len(made),
            out_specs=(hbm,) * len(made),
            scratch_shapes=[vmem(a.shape, a.dtype) for a in made] + [dma((2, len(made)))],
            compiler_params=pltpu.CompilerParams(vmem_limit_bytes=KERNEL_VMEM),
            name="hand_over",
        )(*made)
        return input_grads, key_grads, value_grads, gain_grads.reshape(1, width)

    in_specs = (
        P("pipe", None, ("ctx", "tp"), None),
        P("pipe", None, "ctx", "tp"),
        P("pipe", None, "ctx", "tp"),
        P("pipe", None),
        P("pipe", ("ctx", "tp"), None),
        P(None, ("ctx", "tp"), None),
        P(),
    )
    out_specs = (
        P("pipe", None, ("ctx", "tp"), None),
        P("pipe", None, "ctx", "tp"),
        P("pipe", None, "ctx", "tp"),
        P("pipe", None),
    )
    return jax.shard_map(
        on_device, mesh=mesh, in_specs=in_specs, out_specs=out_specs, check_vma=False
    )
```

```python
import functools
import math

import jax
import jax.numpy as jnp
from jax import lax
from jax.experimental import pallas as pl
from jax.experimental.pallas import tpu as pltpu
from jax.sharding import PartitionSpec as P

HD = 128
HALF = 64
EPS = 1e-05
MASKED = -1e30
SCALE = HD ** (-0.5)
EXP2_SCALE = SCALE * math.log2(math.e)
KERNEL_VMEM = 60 << 20
MESH = pl.DeviceIdType.MESH
f32 = jnp.float32
bf16 = jnp.bfloat16


def remote(src, dst, send_sem, recv_sem, device):
    return pltpu.make_async_remote_copy(
        src_ref=src,
        dst_ref=dst,
        send_sem=send_sem,
        recv_sem=recv_sem,
        device_id=device,
        device_id_type=MESH,
    )


def dot_nt(a, b):
    return lax.dot_general(a, b, (((1,), (1,)), ((), ())), preferred_element_type=f32)


def dot_tn(a, b):
    return lax.dot_general(a, b, (((0,), (0,)), ((), ())), preferred_element_type=f32)


def kernel(
    dims,
    x_hbm,
    k_hbm,
    v_hbm,
    gain_hbm,
    w_hbm,
    og_hbm,
    doc_hbm,
    ig_out,
    dk_out,
    dv_out,
    gain_out,
    xrow,
    xh,
    ah,
    invh,
    kv,
    qs,
    dos,
    e_ref,
    dp_ref,
    m_ref,
    l_ref,
    rt_ref,
    dqt,
    dqs,
    gf,
    gb,
    gp,
    gs,
    gz,
    ig,
    cs,
    cr,
    gacc,
    gr,
    res,
    gain_ref,
    doc_ref,
    local_sem,
    small_sem,
    x_s,
    x_r,
    a_s,
    a_r,
    inv_s,
    inv_r,
    kv_s,
    kv_r,
    fw_s,
    gp_s,
    gp_r,
    gz_s,
    gz_r,
    c_s,
    c_r,
    p_s,
    p_r,
    o_s,
    o_r,
    g_s,
    g_r,
    h_s,
    h_r,
):
    n_pipe, n_ctx, n_tp, ticks, group, docs = dims
    n = n_ctx
    rows = 2 * HALF // n_tp
    cols = group * HD
    width = n_tp * cols
    lanes = group * HALF
    chunk = 256
    pairs = (n + 2) // 2

    seg = lax.axis_index("pipe")
    me = lax.axis_index("ctx")
    tp = lax.axis_index("tp")
    last = n_pipe - 1
    low_pairs = (me + 2) // 2
    high_first = 2 * low_pairs

    def ctx_peer(d):
        return lax.rem(me + d, n)

    def ctx_behind(d):
        return lax.rem(me + n - d, n)

    def tp_peer(d):
        return lax.rem(tp + d, n_tp)

    line = lax.rem(me, 2)
    partner = me + 1 - 2 * line
    lines = n // 2
    far_first = sorted(range(1, lines), key=lambda i: -min(i, lines - i))

    def upper(d):
        return (n + d - 1 - me) // n

    def slot_of(d):
        return (1 - upper(d)) * d + upper(d) * (high_first + n - d)

    def partner_slot(slot, is_upper):
        return slot + (1 - 2 * line) * (1 - 2 * is_upper)

    own_rows = pl.ds(pl.multiple_of(tp * rows, rows), rows)
    own_cols = pl.ds(pl.multiple_of(tp * cols, cols), cols)

    def kv_copies(t):
        return [
            pltpu.make_async_copy(
                ref.at[0, t, pl.ds(i * HALF, HALF)], kv.at[t, slot, which], local_sem.at[t, 2 * which + i]
            )
            for which, ref in enumerate((k_hbm, v_hbm))
            for i, slot in enumerate((0, high_first))
        ]

    def x_copy(t):
        return pltpu.make_async_copy(x_hbm.at[0, t], xrow.at[t], local_sem.at[t, 4])

    def own_x(t):
        return pltpu.make_async_copy(
            x_hbm.at[0, t, :, own_cols], xh.at[t, own_rows, :], local_sem.at[t, 5]
        )

    def own_a(t):
        return pltpu.make_async_copy(
            w_hbm.at[0, :, own_cols], ah.at[t, own_rows, :], local_sem.at[t, 6]
        )

    def own_output_grad(t):
        return pltpu.make_async_copy(
            og_hbm.at[t - 1, :, own_cols], ah.at[t, own_rows, :], local_sem.at[t, 6]
        )

    own_gain = pl.ds(pl.multiple_of(tp * group, group), group)
    small_copies = (
        pltpu.make_async_copy(gain_hbm.at[own_gain, :], gain_ref, small_sem.at[0]),
        pltpu.make_async_copy(doc_hbm, doc_ref, small_sem.at[1]),
    )
    for t in range(ticks):
        for c in kv_copies(t):
            c.start()
    for c in small_copies:
        c.start()
    for t in range(ticks):
        x_copy(t).start()
        own_x(t).start()
        if t == 0:
            own_a(t).start()
        else:

            @pl.when(seg == last)
            def _(t=t):
                own_output_grad(t).start()

    barrier = pltpu.get_barrier_semaphore()

    pl.semaphore_signal(barrier, inc=1, device_id={"ctx": partner}, device_id_type=MESH)
    for i in far_first:
        pl.semaphore_signal(barrier, inc=1, device_id={"ctx": ctx_peer(2 * i)}, device_id_type=MESH)
    for d in range(1, n_tp):
        pl.semaphore_signal(barrier, inc=1, device_id={"tp": tp_peer(d)}, device_id_type=MESH)
    pl.semaphore_signal(
        barrier, inc=1, device_id={"pipe": lax.rem(seg + 1, n_pipe)}, device_id_type=MESH
    )
    pl.semaphore_signal(
        barrier, inc=1, device_id={"pipe": lax.rem(seg + n_pipe - 1, n_pipe)}, device_id_type=MESH
    )

    odd = lax.rem(me, 2)
    pad_slot = (1 - odd) * (me + 1) + odd * (n + 1)
    for t in range(ticks):
        kv[t, pad_slot] = jnp.zeros((2, HALF, HD), bf16)
    for t in range(ticks):
        for c in kv_copies(t):
            c.wait()

    pl.semaphore_wait(barrier, lines + n_tp - 1 + 2)

    def x_send(t, d):
        to = tp_peer(d)
        there = pl.ds(pl.multiple_of(to * cols, cols), cols)
        return remote(
            x_hbm.at[0, t, :, there], xh.at[t, own_rows, :], x_s.at[t, d], x_r.at[t, d], {"tp": to}
        )

    def a_send(t, d):
        to = tp_peer(d)
        there = pl.ds(pl.multiple_of(to * cols, cols), cols)
        src = w_hbm.at[0, :, there] if t == 0 else og_hbm.at[t - 1, :, there]
        return remote(src, ah.at[t, own_rows, :], a_s.at[t, d], a_r.at[t, d], {"tp": to})

    def inv_send(t, d):
        to = tp_peer(d)
        return remote(
            invh.at[t, own_rows, :],
            invh.at[t, own_rows, :],
            inv_s.at[t, d],
            inv_r.at[t, d],
            {"tp": to},
        )

    def kv_send(t, which, i):
        d = 2 * i
        to = ctx_peer(d)
        wrapped = (me + d) // n
        slot = (1 - wrapped) * d + wrapped * (2 * ((to + 2) // 2) + n - d)
        return remote(
            kv.at[t, wrapped * high_first, which],
            kv.at[t, slot, which],
            kv_s.at[t, which, i],
            kv_r.at[t, which, slot],
            {"ctx": to},
        )

    def kv_forward(t, which, i):
        if i == 0:
            slot, is_upper = line * high_first, line
        else:
            slot, is_upper = slot_of(2 * i), upper(2 * i)
        there = partner_slot(slot, is_upper)
        return remote(
            kv.at[t, slot, which],
            kv.at[t, there, which],
            fw_s.at[t, which, i],
            kv_r.at[t, which, there],
            {"ctx": partner},
        )

    def kv_wait(t, which, slot):
        came = kv.at[t, slot, which]
        remote(
            came, came, kv_s.at[t, which, 0], kv_r.at[t, which, slot], {"ctx": partner}
        ).wait_recv()

    def send_kv(t, which):
        kv_forward(t, which, 0).start()
        for i in far_first:
            kv_send(t, which, i).start()

    def forward_kv(t, which):
        for i in far_first:
            kv_wait(t, which, slot_of(2 * i))
            kv_forward(t, which, i).start()

    def inverse(t):
        x_copy(t).wait()
        total = jnp.zeros((rows, HD), f32)
        for c in range(width // HD):
            x = xrow[t, :, c * HD : (c + 1) * HD].astype(f32)
            total = total + x * x
        mean = jnp.sum(total, axis=1, keepdims=True) * (1.0 / width)
        invh[t, own_rows, :] = jnp.broadcast_to(lax.rsqrt(mean + EPS), (rows, HD))
        for d in range(1, n_tp):
            inv_send(t, d).start()

    for t in range(ticks):
        for which in range(2):
            send_kv(t, which)
        inverse(t)
        for d in range(1, n_tp):
            x_send(t, d).start()
        for d in range(1, n_tp):
            if t == 0:
                a_send(t, d).start()
            else:

                @pl.when(seg == last)
                def _(t=t, d=d):
                    a_send(t, d).start()

    def gain_of(g):
        return gain_ref[g : g + 1, :]

    def half_rows(h):
        return slice(h * HALF, (h + 1) * HALF)

    def head_cols(g):
        return slice(g * HD, (g + 1) * HD)

    def normed_of(t, h, g):
        return xh[t, half_rows(h), head_cols(g)].astype(f32) * invh[t, half_rows(h), :]

    def head_rows(g):
        return slice(g * HALF, (g + 1) * HALF)

    def prepare_queries(t, h):
        for g in range(group):
            qs[t, h, head_rows(g), :] = (normed_of(t, h, g) * gain_of(g)).astype(bf16)

    def prepare_arriving(t, h):
        for g in range(group):
            dos[h, head_rows(g), :] = ah[t, half_rows(h), head_cols(g)]

    unroll = pairs

    def each_group(step):
        @pl.loop(0, pairs // unroll)
        def _(i):
            step([i * unroll + u for u in range(unroll)])

    def half_of(p):
        return (p - low_pairs + n) // n

    def pair_of(t, p, which):
        return kv[t, pl.ds(2 * p, 2), which].reshape(2 * HALF, HD)

    chunks = [slice(c * chunk, (c + 1) * chunk) for c in range(lanes // chunk)]

    def wait_forwarded(t, which, p):
        h = half_of(p)

        @pl.when(2 * p + 1 < (1 - h) * (me + 1) + h * (high_first + n - me))
        def _():
            kv_wait(t, which, 2 * p + 1)

    def by_half(values, combine, empty):
        result = [jnp.full((1, lanes), empty, f32) for _ in range(2)]
        for p, value in enumerate(values):
            is_low = p < low_pairs
            result[0] = combine(result[0], jnp.where(is_low, value, empty))
            result[1] = combine(result[1], jnp.where(is_low, empty, value))
        return result

    def softmax(t):
        within = lax.rem(lax.broadcasted_iota(jnp.int32, (1, lanes), 1), HALF)
        low_pos = within + HALF * me
        low_start = jnp.zeros((1, lanes), jnp.int32)
        closing = jnp.int32(0)
        for k in range(docs):
            length = doc_ref[seg + t, k]
            closing = closing + length
            low_start = low_start + jnp.where(closing <= low_pos, length, 0)
        row = lax.broadcasted_iota(jnp.int32, (2 * HALF, chunk), 0)
        row = jnp.where(row < HALF, row, row - 2 * HALF)

        def step(group_pairs):
            for p in group_pairs:
                wait_forwarded(t, 0, p)
            for p in group_pairs:
                h = half_of(p)
                section = (1 - h) * me + h * (2 * n - 1 - me)
                base = HALF * (section - (2 * p - h * high_first))
                up_to = within + (HALF * section - base)
                down_to = jnp.where(h == 0, low_start, HALF * n) - base
                key_pair = pair_of(t, p, 0)
                for at in chunks:
                    s = dot_nt(key_pair, qs[t, h, at, :])
                    s = jnp.where((row <= up_to[:, at]) & (row >= down_to[:, at]), s, MASKED)
                    peak = jnp.max(s, axis=0, keepdims=True)
                    e = jnp.exp2((s - peak) * EXP2_SCALE)
                    m_ref[t, p, :, at] = peak
                    l_ref[p, :, at] = jnp.sum(e, axis=0, keepdims=True)
                    e_ref[t, p, :, at] = e

        each_group(step)
        peaks = [m_ref[t, p] for p in range(pairs)]
        peak = by_half(peaks, jnp.maximum, MASKED)
        alphas = [
            jnp.exp2((m - jnp.where(p < low_pairs, peak[0], peak[1])) * EXP2_SCALE)
            for p, m in enumerate(peaks)
        ]
        total = by_half([a * l_ref[p] for p, a in enumerate(alphas)], jnp.add, 0.0)
        inverse_total = [1.0 / part for part in total]
        for p, alpha in enumerate(alphas):
            m_ref[t, p] = alpha * jnp.where(p < low_pairs, inverse_total[0], inverse_total[1])

    def put_gradient(t, p, which, value):
        value = value.reshape(2, HALF, HD)
        gf[t, pl.ds(2 * p, 2), which] = value
        gb[t, pl.ds(2 * p, 2), which] = value.astype(bf16)

    def values_pass(t):
        def step(group_pairs):
            for p in group_pairs:
                wait_forwarded(t, 1, p)
            for p in group_pairs:
                h = half_of(p)
                value_pair = pair_of(t, p, 1)
                dv = jnp.zeros((2 * HALF, HD), f32)
                for at in chunks:
                    grads = dos[h, at, :]
                    probs = e_ref[t, p, :, at] * m_ref[t, p, :, at]
                    dp = dot_nt(value_pair, grads)
                    dv = dv + jnp.dot(probs.astype(bf16), grads, preferred_element_type=f32)
                    l_ref[p, :, at] = jnp.sum(probs * dp, axis=0, keepdims=True)
                    dp_ref[p, :, at] = dp
                put_gradient(t, p, 1, dv)

        each_group(step)
        terms = by_half([l_ref[p] for p in range(pairs)], jnp.add, 0.0)
        for h in range(2):
            rt_ref[h] = terms[h]

    def keys_pass(t):
        for h in range(2):
            dqt[h] = jnp.zeros((HD, lanes), f32)

        def step(group_pairs):
            for p in group_pairs:
                h = half_of(p)
                key_pair = pair_of(t, p, 0)
                dk = jnp.zeros((2 * HALF, HD), f32)
                for at in chunks:
                    probs = e_ref[t, p, :, at] * m_ref[t, p, :, at]
                    dscore = (probs * (dp_ref[p, :, at] - rt_ref[h, :, at])).astype(bf16)
                    dk = dk + jnp.dot(dscore, qs[t, h, at, :], preferred_element_type=f32)
                    dqt[h, :, at] += dot_tn(key_pair, dscore)
                put_gradient(t, p, 0, dk * SCALE)

        each_group(step)

    def partner_send(t, which, i):
        d = 2 * i + 1
        slot = slot_of(d)
        there = partner_slot(slot, upper(d))
        return remote(
            gb.at[t, slot, which],
            gp.at[t, there, which],
            gp_s.at[t, which, i],
            gp_r.at[t, which, there],
            {"ctx": partner},
        )

    def send_to_partner(t, which):
        @pl.loop(0, lines)
        def _(i):
            partner_send(t, which, i).start()

    def partner_wait(t, which, slot):
        came = gp.at[t, slot, which]
        remote(
            came, came, gp_s.at[t, which, 0], gp_r.at[t, which, slot], {"ctx": partner}
        ).wait_recv()

    def owner_send(t, which, i):
        return remote(
            gs.at[t, i, which],
            gz.at[t, i, which],
            gz_s.at[t, which, i],
            gz_r.at[t, which, i],
            {"ctx": ctx_behind(2 * i)},
        )

    def send_to_owners(t, which):
        for i in far_first:
            slot = slot_of(2 * i)
            partner_wait(t, which, slot)
            both = gf[t, slot, which] + gp[t, slot, which].astype(f32)
            gs[t, i, which] = both.astype(bf16)
            owner_send(t, which, i).start()

    def coupling_send(t, h, d):
        return remote(
            cs.at[t, h], cr.at[t, h, d], c_s.at[t, h, d], c_r.at[t, h, d], {"tp": tp_peer(d)}
        )

    diagonal = lax.broadcasted_iota(jnp.int32, (HALF, HD), 0) == lax.broadcasted_iota(
        jnp.int32, (HALF, HD), 1
    )

    def couple(t, h):
        dq = jnp.transpose(dqt[h] * SCALE)
        low = dq.astype(bf16)
        dqs[h] = low
        part = jnp.zeros((HALF, HD), f32)
        for g in range(group):
            rounded = low[g * HALF : (g + 1) * HALF, :].astype(f32)
            product = rounded * normed_of(t, h, g)
            gacc[pl.ds(g, 1), :] += jnp.sum(product, axis=0, keepdims=True)
            part = part + product * gain_of(g)
        part = jnp.sum(part, axis=1, keepdims=True)
        cs[t, h] = jnp.sum(jnp.where(diagonal, part, 0.0), axis=0, keepdims=True)
        for d in range(1, n_tp):
            coupling_send(t, h, d).start()

    def pipe_send(t, h):
        there = ah.at[t + 1, half_rows(h), :]
        return remote(
            ig.at[t, half_rows(h), :],
            there,
            p_s.at[t, h],
            p_r.at[t, h],
            {"pipe": lax.rem(seg + n_pipe - 1, n_pipe)},
        )

    def out_send(t, j):
        d = lax.rem(j + n_tp - tp, n_tp)
        return remote(
            ig.at[t, j * rows : (j + 1) * rows, :],
            ig_out.at[0, t, :, own_cols],
            o_s.at[t, d],
            o_r.at[t, d],
            {"tp": j},
        )

    def out_own(t):
        return pltpu.make_async_copy(
            ig.at[t, own_rows, :], ig_out.at[0, t, :, own_cols], o_s.at[t, 0]
        )

    per_half = n_tp // 2

    def finish(t, h):
        total = cs[t, h]
        for d in range(1, n_tp):
            coupling_send(t, h, d).wait_recv()
            total = total + cr[t, h, d]
        coupling = jnp.sum(jnp.where(diagonal, total, 0.0), axis=1, keepdims=True) * (1.0 / width)
        for g in range(group):
            normed = normed_of(t, h, g)
            scaled = dqs[h, g * HALF : (g + 1) * HALF, :].astype(f32) * gain_of(g)
            arriving = ah[t, half_rows(h), head_cols(g)].astype(f32)
            result = arriving + invh[t, half_rows(h), :] * (scaled - normed * coupling)
            ig[t, half_rows(h), head_cols(g)] = result.astype(bf16)
        if t + 1 < ticks:

            @pl.when(seg > 0)
            def _():
                pipe_send(t, h).start()

        for j in range(h * per_half, (h + 1) * per_half):

            @pl.when(tp != j)
            def _(j=j):
                out_send(t, j).start()

            @pl.when(tp == j)
            def _():
                out_own(t).start()

    gacc[...] = jnp.zeros((group, HD), f32)

    def wait_rows(t):
        own_x(t).wait()
        for d in range(1, n_tp):
            inv_send(t, d).wait_recv()
            x_send(t, d).wait_recv()

    def wait_arriving(t, h):
        if t == 0:
            if h == 0:
                own_a(t).wait()
                for d in range(1, n_tp):
                    a_send(t, d).wait_recv()
            return

        @pl.when(seg < last)
        def _():
            pipe_send(t - 1, h).wait_recv()

        if h == 0:

            @pl.when(seg == last)
            def _():
                own_output_grad(t).wait()
                for d in range(1, n_tp):
                    a_send(t, d).wait_recv()

    def queries(t):
        wait_rows(t)
        for h in range(2):
            prepare_queries(t, h)

    def values(t):
        for h in range(2):
            wait_arriving(t, h)
            prepare_arriving(t, h)
        values_pass(t)

    def gain_send(i):
        return remote(gacc, gr.at[i], g_s.at[i], g_r.at[i], {"ctx": ctx_peer(2 * i)})

    def gain_of_line():
        total = gacc[...]
        for i in range(1, lines):
            gain_send(i).wait_recv()
            total = total + gr[i]
        gr[0] = total
        gain_across.start()

    gain_across = remote(gr.at[0], gr.at[lines], g_s.at[0], g_r.at[0], {"ctx": partner})

    def gain_share(d):
        return remote(
            gr.at[lines + 1], gain_out.at[own_gain, :], h_s.at[d], h_r.at[d], {"tp": tp_peer(d)}
        )

    for which in range(2):
        forward_kv(0, which)
    for c in small_copies:
        c.wait()
    queries(0)
    softmax(0)
    for which in range(2):
        forward_kv(1, which)
    values(0)
    keys_pass(0)
    for h in range(2):
        couple(0, h)
    queries(1)
    for h in range(2):
        finish(0, h)
    for which in range(2):
        send_to_partner(0, which)
    softmax(1)
    values(1)
    send_to_partner(1, 1)
    for which in range(2):
        send_to_owners(0, which)
    keys_pass(1)
    send_to_partner(1, 0)
    for h in range(2):
        couple(1, h)

    for i in far_first:
        gain_send(i).start()
    send_to_owners(1, 1)
    for h in range(2):
        finish(1, h)
    send_to_owners(1, 0)
    gain_of_line()
    gain_across.wait_recv()
    gr[lines + 1] = gr[0] + gr[lines]
    own_gain_copy = pltpu.make_async_copy(
        gr.at[lines + 1], gain_out.at[own_gain, :], h_s.at[0]
    )
    own_gain_copy.start()
    for d in range(1, n_tp):
        gain_share(d).start()

    def result_copy(t, which):
        out = (dk_out, dv_out)[which]
        return pltpu.make_async_copy(res.at[t, which], out.at[0, t], local_sem.at[t, which])

    for t in range(ticks):
        for which in (1, 0):
            partner_wait(t, which, line * high_first)
            for i, mine in enumerate((0, high_first)):
                middle = (n + 1 - me) // 2
                begin, end = (1, middle) if i == 0 else (middle, lines)
                from_partner = jnp.where(line == i, gp[t, mine, which].astype(f32), 0.0)

                def add(k, total, t=t, which=which):
                    owner_send(t, which, k).wait_recv()
                    return total + gz[t, k, which].astype(f32)

                res[t, which, half_rows(i), :] = lax.fori_loop(
                    begin, end, add, gf[t, mine, which] + from_partner
                )
            result_copy(t, which).start()

    for t in range(ticks):
        for d in range(1, n_tp):
            inv_send(t, d).wait_send()
            x_send(t, d).wait_send()
            if t == 0:
                a_send(t, d).wait_send()
            else:

                @pl.when(seg == last)
                def _(t=t, d=d):
                    a_send(t, d).wait_send()

            for h in range(2):
                coupling_send(t, h, d).wait_send()

        for which in range(2):
            for i in range(lines):
                kv_forward(t, which, i).wait_send()
                if i > 0:
                    kv_send(t, which, i).wait_send()
                    owner_send(t, which, i).wait_send()

            @pl.loop(0, lines)
            def _(i, t=t, which=which):
                partner_send(t, which, i).wait_send()

            result_copy(t, which).wait()

        if t + 1 < ticks:
            for h in range(2):

                @pl.when(seg > 0)
                def _(t=t, h=h):
                    pipe_send(t, h).wait_send()

        for j in range(n_tp):

            @pl.when(tp != j)
            def _(t=t, j=j):
                out_send(t, j).wait_send()

            @pl.when(tp == j)
            def _(t=t):
                out_own(t).wait()

        for d in range(1, n_tp):
            came = ig_out.at[0, t, :, own_cols]
            remote(came, came, o_s.at[t, d], o_r.at[t, d], {"tp": tp_peer(d)}).wait_recv()
    for i in far_first:
        gain_send(i).wait_send()
    gain_across.wait_send()
    own_gain_copy.wait()

    for d in range(1, n_tp):
        gain_share(d).wait_send()
        gain_share(d).wait_recv()


def hand_over(*refs):
    *refs, sems = refs
    count = len(refs) // 3
    came, left, held = refs[:count], refs[count : 2 * count], refs[2 * count :]
    loads = [pltpu.make_async_copy(came[i], held[i], sems.at[0, i]) for i in range(count)]
    stores = [pltpu.make_async_copy(held[i], left[i], sems.at[1, i]) for i in range(count)]
    for c in loads:
        c.start()
    for load, store in zip(loads, stores):
        load.wait()
        store.start()
    for c in stores:
        c.wait()


def solution(mesh):
    n_pipe, n_ctx, n_tp = (mesh.shape[a] for a in ("pipe", "ctx", "tp"))

    def on_device(segment_inputs, keys, values, norm_gain, waiting_grads, output_grads, doc_lengths):
        ticks, rows, width = segment_inputs.shape[1:]
        cols = width // n_tp
        group = cols // HD
        docs = doc_lengths.shape[1]
        lanes = group * HALF
        slots = n_ctx + 2
        pairs = slots // 2
        dims = (n_pipe, n_ctx, n_tp, ticks, group, docs)
        dma = pltpu.SemaphoreType.DMA
        vmem = pltpu.VMEM
        hbm = pl.BlockSpec(memory_space=pl.ANY)
        lines = n_ctx // 2
        scratch = [
            vmem((ticks, rows, width), bf16),
            vmem((ticks, 2 * HALF, cols), bf16),
            vmem((ticks, 2 * HALF, cols), bf16),
            vmem((ticks, 2 * HALF, HD), f32),
            vmem((ticks, slots, 2, HALF, HD), bf16),
            vmem((ticks, 2, lanes, HD), bf16),
            vmem((2, lanes, HD), bf16),
            vmem((ticks, pairs, 2 * HALF, lanes), f32),
            vmem((pairs, 2 * HALF, lanes), f32),
            vmem((ticks, pairs, 1, lanes), f32),
            vmem((pairs, 1, lanes), f32),
            vmem((2, 1, lanes), f32),
            vmem((2, HD, lanes), f32),
            vmem((2, lanes, HD), bf16),
            vmem((ticks, slots, 2, HALF, HD), f32),
            vmem((ticks, slots, 2, HALF, HD), bf16),
            vmem((ticks, slots, 2, HALF, HD), bf16),
            vmem((ticks, lines, 2, HALF, HD), bf16),
            vmem((ticks, lines, 2, HALF, HD), bf16),
            vmem((ticks, 2 * HALF, cols), bf16),
            vmem((ticks, 2, 1, HD), f32),
            vmem((ticks, 2, n_tp, 1, HD), f32),
            vmem((group, HD), f32),
            vmem((lines + 2, group, HD), f32),
            vmem((ticks, 2, 2 * HALF, HD), f32),
            vmem((group, HD), f32),
            pltpu.SMEM(doc_lengths.shape, jnp.int32),
            dma((ticks, 7)),
            dma((2,)),
            dma((ticks, n_tp)),
            dma((ticks, n_tp)),
            dma((ticks, n_tp)),
            dma((ticks, n_tp)),
            dma((ticks, n_tp)),
            dma((ticks, n_tp)),
            dma((ticks, 2, lines)),
            dma((ticks, 2, slots)),
            dma((ticks, 2, lines)),
            dma((ticks, 2, lines)),
            dma((ticks, 2, slots)),
            dma((ticks, 2, lines)),
            dma((ticks, 2, lines)),
            dma((ticks, 2, n_tp)),
            dma((ticks, 2, n_tp)),
            dma((ticks, 2)),
            dma((ticks, 2)),
            dma((ticks, n_tp)),
            dma((ticks, n_tp)),
            dma((lines,)),
            dma((lines,)),
            dma((n_tp,)),
            dma((n_tp,)),
        ]
        input_grads, key_grads, value_grads, gain_grads = pl.pallas_call(
            functools.partial(kernel, dims),
            out_shape=(
                jax.ShapeDtypeStruct((1, ticks, rows, width), bf16),
                jax.ShapeDtypeStruct((1, ticks, 2 * HALF, HD), f32),
                jax.ShapeDtypeStruct((1, ticks, 2 * HALF, HD), f32),
                jax.ShapeDtypeStruct((width // HD, HD), f32),
            ),
            in_specs=[
                hbm,
                hbm,
                hbm,
                hbm,
                hbm,
                hbm,
                hbm,
            ],
            out_specs=(hbm,) * 4,
            scratch_shapes=scratch,
            compiler_params=pltpu.CompilerParams(
                collective_id=0, has_side_effects=True, vmem_limit_bytes=KERNEL_VMEM
            ),
            name="window",
        )(
            segment_inputs,
            keys,
            values,
            norm_gain.reshape(width // HD, HD),
            waiting_grads,
            output_grads,
            doc_lengths,
        )
        made = (input_grads, key_grads, value_grads, gain_grads)
        input_grads, key_grads, value_grads, gain_grads = pl.pallas_call(
            hand_over,
            out_shape=tuple(jax.ShapeDtypeStruct(a.shape, a.dtype) for a in made),
            in_specs=[hbm] * len(made),
            out_specs=(hbm,) * len(made),
            scratch_shapes=[vmem(a.shape, a.dtype) for a in made] + [dma((2, len(made)))],
            compiler_params=pltpu.CompilerParams(vmem_limit_bytes=KERNEL_VMEM),
            name="hand_over",
        )(*made)
        return input_grads, key_grads, value_grads, gain_grads.reshape(1, width)

    in_specs = (
        P("pipe", None, ("ctx", "tp"), None),
        P("pipe", None, "ctx", "tp"),
        P("pipe", None, "ctx", "tp"),
        P("pipe", None),
        P("pipe", ("ctx", "tp"), None),
        P(None, ("ctx", "tp"), None),
        P(),
    )
    out_specs = (
        P("pipe", None, ("ctx", "tp"), None),
        P("pipe", None, "ctx", "tp"),
        P("pipe", None, "ctx", "tp"),
        P("pipe", None),
    )
    return jax.shard_map(
        on_device, mesh=mesh, in_specs=in_specs, out_specs=out_specs, check_vma=False
    )
```

```python
import functools
import math

import jax
import jax.numpy as jnp
from jax import lax
from jax.experimental import pallas as pl
from jax.experimental.pallas import tpu as pltpu
from jax.sharding import PartitionSpec as P

HD = 128
HALF = 64
EPS = 1e-05
MASKED = -1e30
SCALE = HD ** (-0.5)
EXP2_SCALE = SCALE * math.log2(math.e)
KERNEL_VMEM = 60 << 20
MESH = pl.DeviceIdType.MESH
f32 = jnp.float32
bf16 = jnp.bfloat16


def remote(src, dst, send_sem, recv_sem, device):
    return pltpu.make_async_remote_copy(
        src_ref=src,
        dst_ref=dst,
        send_sem=send_sem,
        recv_sem=recv_sem,
        device_id=device,
        device_id_type=MESH,
    )


def dot_nt(a, b):
    return lax.dot_general(a, b, (((1,), (1,)), ((), ())), preferred_element_type=f32)


def dot_tn(a, b):
    return lax.dot_general(a, b, (((0,), (0,)), ((), ())), preferred_element_type=f32)


def kernel(
    dims,
    x_hbm,
    k_hbm,
    v_hbm,
    gain_hbm,
    w_hbm,
    og_hbm,
    doc_hbm,
    ig_out,
    dk_out,
    dv_out,
    gain_out,
    xrow,
    xh,
    ah,
    invh,
    kv,
    qs,
    dos,
    e_ref,
    dp_ref,
    m_ref,
    l_ref,
    rt_ref,
    dqt,
    dqs,
    gf,
    gb,
    gp,
    gs,
    gz,
    ig,
    cs,
    cr,
    gacc,
    gr,
    res,
    gain_ref,
    doc_ref,
    local_sem,
    small_sem,
    x_s,
    x_r,
    a_s,
    a_r,
    inv_s,
    inv_r,
    kv_s,
    kv_r,
    fw_s,
    gp_s,
    gp_r,
    gz_s,
    gz_r,
    c_s,
    c_r,
    p_s,
    p_r,
    o_s,
    o_r,
    g_s,
    g_r,
    h_s,
    h_r,
):
    n_pipe, n_ctx, n_tp, ticks, group, docs = dims
    n = n_ctx
    rows = 2 * HALF // n_tp
    cols = group * HD
    width = n_tp * cols
    lanes = group * HALF
    chunk = 256
    pairs = (n + 2) // 2

    seg = lax.axis_index("pipe")
    me = lax.axis_index("ctx")
    tp = lax.axis_index("tp")
    last = n_pipe - 1
    low_pairs = (me + 2) // 2
    high_first = 2 * low_pairs

    def ctx_peer(d):
        return lax.rem(me + d, n)

    def ctx_behind(d):
        return lax.rem(me + n - d, n)

    def tp_peer(d):
        return lax.rem(tp + d, n_tp)

    line = lax.rem(me, 2)
    partner = me + 1 - 2 * line
    lines = n // 2
    far_first = sorted(range(1, lines), key=lambda i: -min(i, lines - i))

    def upper(d):
        return (n + d - 1 - me) // n

    def slot_of(d):
        return (1 - upper(d)) * d + upper(d) * (high_first + n - d)

    def partner_slot(slot, is_upper):
        return slot + (1 - 2 * line) * (1 - 2 * is_upper)

    own_rows = pl.ds(pl.multiple_of(tp * rows, rows), rows)
    own_cols = pl.ds(pl.multiple_of(tp * cols, cols), cols)

    def kv_copies(t):
        return [
            pltpu.make_async_copy(
                ref.at[0, t, pl.ds(i * HALF, HALF)], kv.at[t, slot, which], local_sem.at[t, 2 * which + i]
            )
            for which, ref in enumerate((k_hbm, v_hbm))
            for i, slot in enumerate((0, high_first))
        ]

    def x_copy(t):
        return pltpu.make_async_copy(x_hbm.at[0, t], xrow.at[t], local_sem.at[t, 4])

    def own_x(t):
        return pltpu.make_async_copy(
            x_hbm.at[0, t, :, own_cols], xh.at[t, own_rows, :], local_sem.at[t, 5]
        )

    def own_a(t):
        return pltpu.make_async_copy(
            w_hbm.at[0, :, own_cols], ah.at[t, own_rows, :], local_sem.at[t, 6]
        )

    def own_output_grad(t):
        return pltpu.make_async_copy(
            og_hbm.at[t - 1, :, own_cols], ah.at[t, own_rows, :], local_sem.at[t, 6]
        )

    own_gain = pl.ds(pl.multiple_of(tp * group, group), group)
    small_copies = (
        pltpu.make_async_copy(gain_hbm.at[own_gain, :], gain_ref, small_sem.at[0]),
        pltpu.make_async_copy(doc_hbm, doc_ref, small_sem.at[1]),
    )
    for t in range(ticks):
        for c in kv_copies(t):
            c.start()
    for c in small_copies:
        c.start()
    for t in range(ticks):
        x_copy(t).start()
        own_x(t).start()
        if t == 0:
            own_a(t).start()
        else:

            @pl.when(seg == last)
            def _(t=t):
                own_output_grad(t).start()

    barrier = pltpu.get_barrier_semaphore()

    pl.semaphore_signal(barrier, inc=1, device_id={"ctx": partner}, device_id_type=MESH)
    for i in far_first:
        pl.semaphore_signal(barrier, inc=1, device_id={"ctx": ctx_peer(2 * i)}, device_id_type=MESH)
    for d in range(1, n_tp):
        pl.semaphore_signal(barrier, inc=1, device_id={"tp": tp_peer(d)}, device_id_type=MESH)
    pl.semaphore_signal(
        barrier, inc=1, device_id={"pipe": lax.rem(seg + 1, n_pipe)}, device_id_type=MESH
    )
    pl.semaphore_signal(
        barrier, inc=1, device_id={"pipe": lax.rem(seg + n_pipe - 1, n_pipe)}, device_id_type=MESH
    )

    odd = lax.rem(me, 2)
    pad_slot = (1 - odd) * (me + 1) + odd * (n + 1)
    for t in range(ticks):
        kv[t, pad_slot] = jnp.zeros((2, HALF, HD), bf16)
    for t in range(ticks):
        for c in kv_copies(t):
            c.wait()

    pl.semaphore_wait(barrier, lines + n_tp - 1 + 2)

    def x_send(t, d):
        to = tp_peer(d)
        there = pl.ds(pl.multiple_of(to * cols, cols), cols)
        return remote(
            x_hbm.at[0, t, :, there], xh.at[t, own_rows, :], x_s.at[t, d], x_r.at[t, d], {"tp": to}
        )

    def a_send(t, d):
        to = tp_peer(d)
        there = pl.ds(pl.multiple_of(to * cols, cols), cols)
        src = w_hbm.at[0, :, there] if t == 0 else og_hbm.at[t - 1, :, there]
        return remote(src, ah.at[t, own_rows, :], a_s.at[t, d], a_r.at[t, d], {"tp": to})

    def inv_send(t, d):
        to = tp_peer(d)
        return remote(
            invh.at[t, own_rows, :],
            invh.at[t, own_rows, :],
            inv_s.at[t, d],
            inv_r.at[t, d],
            {"tp": to},
        )

    def kv_send(t, which, i):
        d = 2 * i
        to = ctx_peer(d)
        wrapped = (me + d) // n
        slot = (1 - wrapped) * d + wrapped * (2 * ((to + 2) // 2) + n - d)
        return remote(
            kv.at[t, wrapped * high_first, which],
            kv.at[t, slot, which],
            kv_s.at[t, which, i],
            kv_r.at[t, which, slot],
            {"ctx": to},
        )

    def kv_forward(t, which, i):
        if i == 0:
            slot, is_upper = line * high_first, line
        else:
            slot, is_upper = slot_of(2 * i), upper(2 * i)
        there = partner_slot(slot, is_upper)
        return remote(
            kv.at[t, slot, which],
            kv.at[t, there, which],
            fw_s.at[t, which, i],
            kv_r.at[t, which, there],
            {"ctx": partner},
        )

    def kv_wait(t, which, slot):
        came = kv.at[t, slot, which]
        remote(
            came, came, kv_s.at[t, which, 0], kv_r.at[t, which, slot], {"ctx": partner}
        ).wait_recv()

    def send_kv(t, which):
        kv_forward(t, which, 0).start()
        for i in far_first:
            kv_send(t, which, i).start()

    def forward_kv(t, which):
        for i in far_first:
            kv_wait(t, which, slot_of(2 * i))
            kv_forward(t, which, i).start()

    def inverse(t):
        x_copy(t).wait()
        total = jnp.zeros((rows, HD), f32)
        for c in range(width // HD):
            x = xrow[t, :, c * HD : (c + 1) * HD].astype(f32)
            total = total + x * x
        mean = jnp.sum(total, axis=1, keepdims=True) * (1.0 / width)
        invh[t, own_rows, :] = jnp.broadcast_to(lax.rsqrt(mean + EPS), (rows, HD))
        for d in range(1, n_tp):
            inv_send(t, d).start()

    for t in range(ticks):
        for which in range(2):
            send_kv(t, which)
        inverse(t)
        for d in range(1, n_tp):
            x_send(t, d).start()
        for d in range(1, n_tp):
            if t == 0:
                a_send(t, d).start()
            else:

                @pl.when(seg == last)
                def _(t=t, d=d):
                    a_send(t, d).start()

    def gain_of(g):
        return gain_ref[g : g + 1, :]

    def half_rows(h):
        return slice(h * HALF, (h + 1) * HALF)

    def head_cols(g):
        return slice(g * HD, (g + 1) * HD)

    def normed_of(t, h, g):
        return xh[t, half_rows(h), head_cols(g)].astype(f32) * invh[t, half_rows(h), :]

    def head_rows(g):
        return slice(g * HALF, (g + 1) * HALF)

    def prepare_queries(t, h):
        for g in range(group):
            qs[t, h, head_rows(g), :] = (normed_of(t, h, g) * gain_of(g)).astype(bf16)

    def prepare_arriving(t, h):
        for g in range(group):
            dos[h, head_rows(g), :] = ah[t, half_rows(h), head_cols(g)]

    unroll = pairs

    def each_group(step):
        @pl.loop(0, pairs // unroll)
        def _(i):
            step([i * unroll + u for u in range(unroll)])

    def half_of(p):
        return (p - low_pairs + n) // n

    def pair_of(t, p, which):
        return kv[t, pl.ds(2 * p, 2), which].reshape(2 * HALF, HD)

    chunks = [slice(c * chunk, (c + 1) * chunk) for c in range(lanes // chunk)]

    def wait_forwarded(t, which, p):
        h = half_of(p)

        @pl.when(2 * p + 1 < (1 - h) * (me + 1) + h * (high_first + n - me))
        def _():
            kv_wait(t, which, 2 * p + 1)

    def by_half(values, combine, empty):
        result = [jnp.full((1, lanes), empty, f32) for _ in range(2)]
        for p, value in enumerate(values):
            is_low = p < low_pairs
            result[0] = combine(result[0], jnp.where(is_low, value, empty))
            result[1] = combine(result[1], jnp.where(is_low, empty, value))
        return result

    def softmax(t):
        within = lax.rem(lax.broadcasted_iota(jnp.int32, (1, lanes), 1), HALF)
        low_pos = within + HALF * me
        low_start = jnp.zeros((1, lanes), jnp.int32)
        closing = jnp.int32(0)
        for k in range(docs):
            length = doc_ref[seg + t, k]
            closing = closing + length
            low_start = low_start + jnp.where(closing <= low_pos, length, 0)
        row = lax.broadcasted_iota(jnp.int32, (2 * HALF, chunk), 0)
        row = jnp.where(row < HALF, row, row - 2 * HALF)

        def step(group_pairs):
            for p in group_pairs:
                wait_forwarded(t, 0, p)
            for p in group_pairs:
                h = half_of(p)
                section = (1 - h) * me + h * (2 * n - 1 - me)
                base = HALF * (section - (2 * p - h * high_first))
                up_to = within + (HALF * section - base)
                down_to = jnp.where(h == 0, low_start, HALF * n) - base
                key_pair = pair_of(t, p, 0)
                for at in chunks:
                    s = dot_nt(key_pair, qs[t, h, at, :])
                    s = jnp.where((row <= up_to[:, at]) & (row >= down_to[:, at]), s, MASKED)
                    peak = jnp.max(s, axis=0, keepdims=True)
                    e = jnp.exp2((s - peak) * EXP2_SCALE)
                    m_ref[t, p, :, at] = peak
                    l_ref[p, :, at] = jnp.sum(e, axis=0, keepdims=True)
                    e_ref[t, p, :, at] = e

        each_group(step)
        peaks = [m_ref[t, p] for p in range(pairs)]
        peak = by_half(peaks, jnp.maximum, MASKED)
        alphas = [
            jnp.exp2((m - jnp.where(p < low_pairs, peak[0], peak[1])) * EXP2_SCALE)
            for p, m in enumerate(peaks)
        ]
        total = by_half([a * l_ref[p] for p, a in enumerate(alphas)], jnp.add, 0.0)
        inverse_total = [1.0 / part for part in total]
        for p, alpha in enumerate(alphas):
            m_ref[t, p] = alpha * jnp.where(p < low_pairs, inverse_total[0], inverse_total[1])

    def put_gradient(t, p, which, value):
        value = value.reshape(2, HALF, HD)
        gf[t, pl.ds(2 * p, 2), which] = value
        gb[t, pl.ds(2 * p, 2), which] = value.astype(bf16)

    def values_pass(t):
        def step(group_pairs):
            for p in group_pairs:
                wait_forwarded(t, 1, p)
            for p in group_pairs:
                h = half_of(p)
                value_pair = pair_of(t, p, 1)
                dv = jnp.zeros((2 * HALF, HD), f32)
                for at in chunks:
                    grads = dos[h, at, :]
                    probs = e_ref[t, p, :, at] * m_ref[t, p, :, at]
                    dp = dot_nt(value_pair, grads)
                    dv = dv + jnp.dot(probs.astype(bf16), grads, preferred_element_type=f32)
                    l_ref[p, :, at] = jnp.sum(probs * dp, axis=0, keepdims=True)
                    dp_ref[p, :, at] = dp
                put_gradient(t, p, 1, dv)

        each_group(step)
        terms = by_half([l_ref[p] for p in range(pairs)], jnp.add, 0.0)
        for h in range(2):
            rt_ref[h] = terms[h]

    def keys_pass(t):
        for h in range(2):
            dqt[h] = jnp.zeros((HD, lanes), f32)

        def step(group_pairs):
            for p in group_pairs:
                h = half_of(p)
                key_pair = pair_of(t, p, 0)
                dk = jnp.zeros((2 * HALF, HD), f32)
                for at in chunks:
                    probs = e_ref[t, p, :, at] * m_ref[t, p, :, at]
                    dscore = (probs * (dp_ref[p, :, at] - rt_ref[h, :, at])).astype(bf16)
                    dk = dk + jnp.dot(dscore, qs[t, h, at, :], preferred_element_type=f32)
                    dqt[h, :, at] += dot_tn(key_pair, dscore)
                put_gradient(t, p, 0, dk * SCALE)

        each_group(step)

    def partner_send(t, which, i):
        d = 2 * i + 1
        slot = slot_of(d)
        there = partner_slot(slot, upper(d))
        return remote(
            gb.at[t, slot, which],
            gp.at[t, there, which],
            gp_s.at[t, which, i],
            gp_r.at[t, which, there],
            {"ctx": partner},
        )

    def send_to_partner(t, which):
        @pl.loop(0, lines)
        def _(i):
            partner_send(t, which, i).start()

    def partner_wait(t, which, slot):
        came = gp.at[t, slot, which]
        remote(
            came, came, gp_s.at[t, which, 0], gp_r.at[t, which, slot], {"ctx": partner}
        ).wait_recv()

    def owner_send(t, which, i):
        return remote(
            gs.at[t, i, which],
            gz.at[t, i, which],
            gz_s.at[t, which, i],
            gz_r.at[t, which, i],
            {"ctx": ctx_behind(2 * i)},
        )

    def send_to_owners(t, which):
        for i in far_first:
            slot = slot_of(2 * i)
            partner_wait(t, which, slot)
            both = gf[t, slot, which] + gp[t, slot, which].astype(f32)
            gs[t, i, which] = both.astype(bf16)
            owner_send(t, which, i).start()

    def coupling_send(t, h, d):
        return remote(
            cs.at[t, h], cr.at[t, h, d], c_s.at[t, h, d], c_r.at[t, h, d], {"tp": tp_peer(d)}
        )

    diagonal = lax.broadcasted_iota(jnp.int32, (HALF, HD), 0) == lax.broadcasted_iota(
        jnp.int32, (HALF, HD), 1
    )

    def couple(t, h):
        dq = jnp.transpose(dqt[h] * SCALE)
        low = dq.astype(bf16)
        dqs[h] = low
        part = jnp.zeros((HALF, HD), f32)
        for g in range(group):
            rounded = low[g * HALF : (g + 1) * HALF, :].astype(f32)
            product = rounded * normed_of(t, h, g)
            gacc[pl.ds(g, 1), :] += jnp.sum(product, axis=0, keepdims=True)
            part = part + product * gain_of(g)
        part = jnp.sum(part, axis=1, keepdims=True)
        cs[t, h] = jnp.sum(jnp.where(diagonal, part, 0.0), axis=0, keepdims=True)
        for d in range(1, n_tp):
            coupling_send(t, h, d).start()

    def pipe_send(t, h):
        there = ah.at[t + 1, half_rows(h), :]
        return remote(
            ig.at[t, half_rows(h), :],
            there,
            p_s.at[t, h],
            p_r.at[t, h],
            {"pipe": lax.rem(seg + n_pipe - 1, n_pipe)},
        )

    def out_send(t, j):
        d = lax.rem(j + n_tp - tp, n_tp)
        return remote(
            ig.at[t, j * rows : (j + 1) * rows, :],
            ig_out.at[0, t, :, own_cols],
            o_s.at[t, d],
            o_r.at[t, d],
            {"tp": j},
        )

    def out_own(t):
        return pltpu.make_async_copy(
            ig.at[t, own_rows, :], ig_out.at[0, t, :, own_cols], o_s.at[t, 0]
        )

    per_half = n_tp // 2

    def finish(t, h):
        total = cs[t, h]
        for d in range(1, n_tp):
            coupling_send(t, h, d).wait_recv()
            total = total + cr[t, h, d]
        coupling = jnp.sum(jnp.where(diagonal, total, 0.0), axis=1, keepdims=True) * (1.0 / width)
        for g in range(group):
            normed = normed_of(t, h, g)
            scaled = dqs[h, g * HALF : (g + 1) * HALF, :].astype(f32) * gain_of(g)
            arriving = ah[t, half_rows(h), head_cols(g)].astype(f32)
            result = arriving + invh[t, half_rows(h), :] * (scaled - normed * coupling)
            ig[t, half_rows(h), head_cols(g)] = result.astype(bf16)
        if t + 1 < ticks:

            @pl.when(seg > 0)
            def _():
                pipe_send(t, h).start()

        for j in range(h * per_half, (h + 1) * per_half):

            @pl.when(tp != j)
            def _(j=j):
                out_send(t, j).start()

            @pl.when(tp == j)
            def _():
                out_own(t).start()

    gacc[...] = jnp.zeros((group, HD), f32)

    def wait_rows(t):
        own_x(t).wait()
        for d in range(1, n_tp):
            inv_send(t, d).wait_recv()
            x_send(t, d).wait_recv()

    def wait_arriving(t, h):
        if t == 0:
            if h == 0:
                own_a(t).wait()
                for d in range(1, n_tp):
                    a_send(t, d).wait_recv()
            return

        @pl.when(seg < last)
        def _():
            pipe_send(t - 1, h).wait_recv()

        if h == 0:

            @pl.when(seg == last)
            def _():
                own_output_grad(t).wait()
                for d in range(1, n_tp):
                    a_send(t, d).wait_recv()

    def queries(t):
        wait_rows(t)
        for h in range(2):
            prepare_queries(t, h)

    def values(t):
        for h in range(2):
            wait_arriving(t, h)
            prepare_arriving(t, h)
        values_pass(t)

    def gain_send(i):
        return remote(gacc, gr.at[i], g_s.at[i], g_r.at[i], {"ctx": ctx_peer(2 * i)})

    def gain_of_line():
        total = gacc[...]
        for i in range(1, lines):
            gain_send(i).wait_recv()
            total = total + gr[i]
        gr[0] = total
        gain_across.start()

    gain_across = remote(gr.at[0], gr.at[lines], g_s.at[0], g_r.at[0], {"ctx": partner})

    def gain_share(d):
        return remote(
            gr.at[lines + 1], gain_out.at[own_gain, :], h_s.at[d], h_r.at[d], {"tp": tp_peer(d)}
        )

    for which in range(2):
        forward_kv(0, which)
    for c in small_copies:
        c.wait()
    queries(0)
    softmax(0)
    for which in range(2):
        forward_kv(1, which)
    values(0)
    keys_pass(0)
    for h in range(2):
        couple(0, h)
    for which in range(2):
        send_to_partner(0, which)
    queries(1)
    for h in range(2):
        finish(0, h)
    softmax(1)
    for which in (1, 0):
        send_to_owners(0, which)
    values(1)
    send_to_partner(1, 1)
    keys_pass(1)
    send_to_partner(1, 0)
    for h in range(2):
        couple(1, h)

    for i in far_first:
        gain_send(i).start()
    send_to_owners(1, 1)
    for h in range(2):
        finish(1, h)
    send_to_owners(1, 0)
    gain_of_line()
    gain_across.wait_recv()
    gr[lines + 1] = gr[0] + gr[lines]
    own_gain_copy = pltpu.make_async_copy(
        gr.at[lines + 1], gain_out.at[own_gain, :], h_s.at[0]
    )
    own_gain_copy.start()
    for d in range(1, n_tp):
        gain_share(d).start()

    def result_copy(t, which):
        out = (dk_out, dv_out)[which]
        return pltpu.make_async_copy(res.at[t, which], out.at[0, t], local_sem.at[t, which])

    for t in range(ticks):
        for which in (1, 0):
            partner_wait(t, which, line * high_first)
            for i, mine in enumerate((0, high_first)):
                middle = (n + 1 - me) // 2
                begin, end = (1, middle) if i == 0 else (middle, lines)
                from_partner = jnp.where(line == i, gp[t, mine, which].astype(f32), 0.0)

                def add(k, total, t=t, which=which):
                    owner_send(t, which, k).wait_recv()
                    return total + gz[t, k, which].astype(f32)

                res[t, which, half_rows(i), :] = lax.fori_loop(
                    begin, end, add, gf[t, mine, which] + from_partner
                )
            result_copy(t, which).start()

    for t in range(ticks):
        for d in range(1, n_tp):
            inv_send(t, d).wait_send()
            x_send(t, d).wait_send()
            if t == 0:
                a_send(t, d).wait_send()
            else:

                @pl.when(seg == last)
                def _(t=t, d=d):
                    a_send(t, d).wait_send()

            for h in range(2):
                coupling_send(t, h, d).wait_send()

        for which in range(2):
            for i in range(lines):
                kv_forward(t, which, i).wait_send()
                if i > 0:
                    kv_send(t, which, i).wait_send()
                    owner_send(t, which, i).wait_send()

            @pl.loop(0, lines)
            def _(i, t=t, which=which):
                partner_send(t, which, i).wait_send()

            result_copy(t, which).wait()

        if t + 1 < ticks:
            for h in range(2):

                @pl.when(seg > 0)
                def _(t=t, h=h):
                    pipe_send(t, h).wait_send()

        for j in range(n_tp):

            @pl.when(tp != j)
            def _(t=t, j=j):
                out_send(t, j).wait_send()

            @pl.when(tp == j)
            def _(t=t):
                out_own(t).wait()

        for d in range(1, n_tp):
            came = ig_out.at[0, t, :, own_cols]
            remote(came, came, o_s.at[t, d], o_r.at[t, d], {"tp": tp_peer(d)}).wait_recv()
    for i in far_first:
        gain_send(i).wait_send()
    gain_across.wait_send()
    own_gain_copy.wait()

    for d in range(1, n_tp):
        gain_share(d).wait_send()
        gain_share(d).wait_recv()


def hand_over(*refs):
    *refs, sems = refs
    count = len(refs) // 3
    came, left, held = refs[:count], refs[count : 2 * count], refs[2 * count :]
    loads = [pltpu.make_async_copy(came[i], held[i], sems.at[0, i]) for i in range(count)]
    stores = [pltpu.make_async_copy(held[i], left[i], sems.at[1, i]) for i in range(count)]
    for c in loads:
        c.start()
    for load, store in zip(loads, stores):
        load.wait()
        store.start()
    for c in stores:
        c.wait()


def solution(mesh):
    n_pipe, n_ctx, n_tp = (mesh.shape[a] for a in ("pipe", "ctx", "tp"))

    def on_device(segment_inputs, keys, values, norm_gain, waiting_grads, output_grads, doc_lengths):
        ticks, rows, width = segment_inputs.shape[1:]
        cols = width // n_tp
        group = cols // HD
        docs = doc_lengths.shape[1]
        lanes = group * HALF
        slots = n_ctx + 2
        pairs = slots // 2
        dims = (n_pipe, n_ctx, n_tp, ticks, group, docs)
        dma = pltpu.SemaphoreType.DMA
        vmem = pltpu.VMEM
        hbm = pl.BlockSpec(memory_space=pl.ANY)
        lines = n_ctx // 2
        scratch = [
            vmem((ticks, rows, width), bf16),
            vmem((ticks, 2 * HALF, cols), bf16),
            vmem((ticks, 2 * HALF, cols), bf16),
            vmem((ticks, 2 * HALF, HD), f32),
            vmem((ticks, slots, 2, HALF, HD), bf16),
            vmem((ticks, 2, lanes, HD), bf16),
            vmem((2, lanes, HD), bf16),
            vmem((ticks, pairs, 2 * HALF, lanes), f32),
            vmem((pairs, 2 * HALF, lanes), f32),
            vmem((ticks, pairs, 1, lanes), f32),
            vmem((pairs, 1, lanes), f32),
            vmem((2, 1, lanes), f32),
            vmem((2, HD, lanes), f32),
            vmem((2, lanes, HD), bf16),
            vmem((ticks, slots, 2, HALF, HD), f32),
            vmem((ticks, slots, 2, HALF, HD), bf16),
            vmem((ticks, slots, 2, HALF, HD), bf16),
            vmem((ticks, lines, 2, HALF, HD), bf16),
            vmem((ticks, lines, 2, HALF, HD), bf16),
            vmem((ticks, 2 * HALF, cols), bf16),
            vmem((ticks, 2, 1, HD), f32),
            vmem((ticks, 2, n_tp, 1, HD), f32),
            vmem((group, HD), f32),
            vmem((lines + 2, group, HD), f32),
            vmem((ticks, 2, 2 * HALF, HD), f32),
            vmem((group, HD), f32),
            pltpu.SMEM(doc_lengths.shape, jnp.int32),
            dma((ticks, 7)),
            dma((2,)),
            dma((ticks, n_tp)),
            dma((ticks, n_tp)),
            dma((ticks, n_tp)),
            dma((ticks, n_tp)),
            dma((ticks, n_tp)),
            dma((ticks, n_tp)),
            dma((ticks, 2, lines)),
            dma((ticks, 2, slots)),
            dma((ticks, 2, lines)),
            dma((ticks, 2, lines)),
            dma((ticks, 2, slots)),
            dma((ticks, 2, lines)),
            dma((ticks, 2, lines)),
            dma((ticks, 2, n_tp)),
            dma((ticks, 2, n_tp)),
            dma((ticks, 2)),
            dma((ticks, 2)),
            dma((ticks, n_tp)),
            dma((ticks, n_tp)),
            dma((lines,)),
            dma((lines,)),
            dma((n_tp,)),
            dma((n_tp,)),
        ]
        input_grads, key_grads, value_grads, gain_grads = pl.pallas_call(
            functools.partial(kernel, dims),
            out_shape=(
                jax.ShapeDtypeStruct((1, ticks, rows, width), bf16),
                jax.ShapeDtypeStruct((1, ticks, 2 * HALF, HD), f32),
                jax.ShapeDtypeStruct((1, ticks, 2 * HALF, HD), f32),
                jax.ShapeDtypeStruct((width // HD, HD), f32),
            ),
            in_specs=[
                hbm,
                hbm,
                hbm,
                hbm,
                hbm,
                hbm,
                hbm,
            ],
            out_specs=(hbm,) * 4,
            scratch_shapes=scratch,
            compiler_params=pltpu.CompilerParams(
                collective_id=0, has_side_effects=True, vmem_limit_bytes=KERNEL_VMEM
            ),
            name="window",
        )(
            segment_inputs,
            keys,
            values,
            norm_gain.reshape(width // HD, HD),
            waiting_grads,
            output_grads,
            doc_lengths,
        )
        made = (input_grads, key_grads, value_grads, gain_grads)
        input_grads, key_grads, value_grads, gain_grads = pl.pallas_call(
            hand_over,
            out_shape=tuple(jax.ShapeDtypeStruct(a.shape, a.dtype) for a in made),
            in_specs=[hbm] * len(made),
            out_specs=(hbm,) * len(made),
            scratch_shapes=[vmem(a.shape, a.dtype) for a in made] + [dma((2, len(made)))],
            compiler_params=pltpu.CompilerParams(vmem_limit_bytes=KERNEL_VMEM),
            name="hand_over",
        )(*made)
        return input_grads, key_grads, value_grads, gain_grads.reshape(1, width)

    in_specs = (
        P("pipe", None, ("ctx", "tp"), None),
        P("pipe", None, "ctx", "tp"),
        P("pipe", None, "ctx", "tp"),
        P("pipe", None),
        P("pipe", ("ctx", "tp"), None),
        P(None, ("ctx", "tp"), None),
        P(),
    )
    out_specs = (
        P("pipe", None, ("ctx", "tp"), None),
        P("pipe", None, "ctx", "tp"),
        P("pipe", None, "ctx", "tp"),
        P("pipe", None),
    )
    return jax.shard_map(
        on_device, mesh=mesh, in_specs=in_specs, out_specs=out_specs, check_vma=False
    )
```

```python
import functools
import math

import jax
import jax.numpy as jnp
from jax import lax
from jax.experimental import pallas as pl
from jax.experimental.pallas import tpu as pltpu
from jax.sharding import PartitionSpec as P

HD = 128
HALF = 64
EPS = 1e-05
MASKED = -1e30
SCALE = HD ** (-0.5)
EXP2_SCALE = SCALE * math.log2(math.e)
KERNEL_VMEM = 60 << 20
MESH = pl.DeviceIdType.MESH
f32 = jnp.float32
bf16 = jnp.bfloat16


def remote(src, dst, send_sem, recv_sem, device):
    return pltpu.make_async_remote_copy(
        src_ref=src,
        dst_ref=dst,
        send_sem=send_sem,
        recv_sem=recv_sem,
        device_id=device,
        device_id_type=MESH,
    )


def dot_nt(a, b):
    return lax.dot_general(a, b, (((1,), (1,)), ((), ())), preferred_element_type=f32)


def dot_tn(a, b):
    return lax.dot_general(a, b, (((0,), (0,)), ((), ())), preferred_element_type=f32)


def kernel(
    dims,
    x_hbm,
    k_hbm,
    v_hbm,
    gain_hbm,
    w_hbm,
    og_hbm,
    doc_hbm,
    ig_out,
    dk_out,
    dv_out,
    gain_out,
    xrow,
    xh,
    ah,
    invh,
    kv,
    qs,
    dos,
    e_ref,
    dp_ref,
    m_ref,
    l_ref,
    rt_ref,
    dqt,
    dqs,
    gf,
    gb,
    gp,
    gs,
    gz,
    ig,
    cs,
    cr,
    gacc,
    gr,
    res,
    gain_ref,
    doc_ref,
    local_sem,
    small_sem,
    x_s,
    x_r,
    a_s,
    a_r,
    inv_s,
    inv_r,
    kv_s,
    kv_r,
    fw_s,
    gp_s,
    gp_r,
    gz_s,
    gz_r,
    c_s,
    c_r,
    p_s,
    p_r,
    o_s,
    o_r,
    g_s,
    g_r,
    h_s,
    h_r,
):
    n_pipe, n_ctx, n_tp, ticks, group, docs = dims
    n = n_ctx
    rows = 2 * HALF // n_tp
    cols = group * HD
    width = n_tp * cols
    lanes = group * HALF
    chunk = 256
    pairs = (n + 2) // 2

    seg = lax.axis_index("pipe")
    me = lax.axis_index("ctx")
    tp = lax.axis_index("tp")
    last = n_pipe - 1
    low_pairs = (me + 2) // 2
    high_first = 2 * low_pairs

    def ctx_peer(d):
        return lax.rem(me + d, n)

    def ctx_behind(d):
        return lax.rem(me + n - d, n)

    def tp_peer(d):
        return lax.rem(tp + d, n_tp)

    line = lax.rem(me, 2)
    partner = me + 1 - 2 * line
    lines = n // 2
    far_first = sorted(range(1, lines), key=lambda i: -min(i, lines - i))

    def upper(d):
        return (n + d - 1 - me) // n

    def slot_of(d):
        return (1 - upper(d)) * d + upper(d) * (high_first + n - d)

    def partner_slot(slot, is_upper):
        return slot + (1 - 2 * line) * (1 - 2 * is_upper)

    own_rows = pl.ds(pl.multiple_of(tp * rows, rows), rows)
    own_cols = pl.ds(pl.multiple_of(tp * cols, cols), cols)

    def kv_copies(t):
        return [
            pltpu.make_async_copy(
                ref.at[0, t, pl.ds(i * HALF, HALF)], kv.at[t, slot, which], local_sem.at[t, 2 * which + i]
            )
            for which, ref in enumerate((k_hbm, v_hbm))
            for i, slot in enumerate((0, high_first))
        ]

    def x_copy(t):
        return pltpu.make_async_copy(x_hbm.at[0, t], xrow.at[t], local_sem.at[t, 4])

    def own_x(t):
        return pltpu.make_async_copy(
            x_hbm.at[0, t, :, own_cols], xh.at[t, own_rows, :], local_sem.at[t, 5]
        )

    def own_a(t):
        return pltpu.make_async_copy(
            w_hbm.at[0, :, own_cols], ah.at[t, own_rows, :], local_sem.at[t, 6]
        )

    def own_output_grad(t):
        return pltpu.make_async_copy(
            og_hbm.at[t - 1, :, own_cols], ah.at[t, own_rows, :], local_sem.at[t, 6]
        )

    own_gain = pl.ds(pl.multiple_of(tp * group, group), group)
    small_copies = (
        pltpu.make_async_copy(gain_hbm.at[own_gain, :], gain_ref, small_sem.at[0]),
        pltpu.make_async_copy(doc_hbm, doc_ref, small_sem.at[1]),
    )
    for t in range(ticks):
        for c in kv_copies(t):
            c.start()
    for c in small_copies:
        c.start()
    for t in range(ticks):
        x_copy(t).start()
        own_x(t).start()
        if t == 0:
            own_a(t).start()
        else:

            @pl.when(seg == last)
            def _(t=t):
                own_output_grad(t).start()

    barrier = pltpu.get_barrier_semaphore()

    pl.semaphore_signal(barrier, inc=1, device_id={"ctx": partner}, device_id_type=MESH)
    for i in far_first:
        pl.semaphore_signal(barrier, inc=1, device_id={"ctx": ctx_peer(2 * i)}, device_id_type=MESH)
    for d in range(1, n_tp):
        pl.semaphore_signal(barrier, inc=1, device_id={"tp": tp_peer(d)}, device_id_type=MESH)
    pl.semaphore_signal(
        barrier, inc=1, device_id={"pipe": lax.rem(seg + 1, n_pipe)}, device_id_type=MESH
    )
    pl.semaphore_signal(
        barrier, inc=1, device_id={"pipe": lax.rem(seg + n_pipe - 1, n_pipe)}, device_id_type=MESH
    )

    odd = lax.rem(me, 2)
    pad_slot = (1 - odd) * (me + 1) + odd * (n + 1)
    for t in range(ticks):
        kv[t, pad_slot] = jnp.zeros((2, HALF, HD), bf16)
    for t in range(ticks):
        for c in kv_copies(t):
            c.wait()

    pl.semaphore_wait(barrier, lines + n_tp - 1 + 2)

    def x_send(t, d):
        to = tp_peer(d)
        there = pl.ds(pl.multiple_of(to * cols, cols), cols)
        return remote(
            x_hbm.at[0, t, :, there], xh.at[t, own_rows, :], x_s.at[t, d], x_r.at[t, d], {"tp": to}
        )

    def a_send(t, d):
        to = tp_peer(d)
        there = pl.ds(pl.multiple_of(to * cols, cols), cols)
        src = w_hbm.at[0, :, there] if t == 0 else og_hbm.at[t - 1, :, there]
        return remote(src, ah.at[t, own_rows, :], a_s.at[t, d], a_r.at[t, d], {"tp": to})

    def inv_send(t, d):
        to = tp_peer(d)
        return remote(
            invh.at[t, own_rows, :],
            invh.at[t, own_rows, :],
            inv_s.at[t, d],
            inv_r.at[t, d],
            {"tp": to},
        )

    def kv_send(t, which, i):
        d = 2 * i
        to = ctx_peer(d)
        wrapped = (me + d) // n
        slot = (1 - wrapped) * d + wrapped * (2 * ((to + 2) // 2) + n - d)
        return remote(
            kv.at[t, wrapped * high_first, which],
            kv.at[t, slot, which],
            kv_s.at[t, which, i],
            kv_r.at[t, which, slot],
            {"ctx": to},
        )

    def kv_forward(t, which, i):
        if i == 0:
            slot, is_upper = line * high_first, line
        else:
            slot, is_upper = slot_of(2 * i), upper(2 * i)
        there = partner_slot(slot, is_upper)
        return remote(
            kv.at[t, slot, which],
            kv.at[t, there, which],
            fw_s.at[t, which, i],
            kv_r.at[t, which, there],
            {"ctx": partner},
        )

    def kv_wait(t, which, slot):
        came = kv.at[t, slot, which]
        remote(
            came, came, kv_s.at[t, which, 0], kv_r.at[t, which, slot], {"ctx": partner}
        ).wait_recv()

    def send_kv(t, which):
        kv_forward(t, which, 0).start()
        for i in far_first:
            kv_send(t, which, i).start()

    def forward_kv(t, which):
        for i in far_first:
            kv_wait(t, which, slot_of(2 * i))
            kv_forward(t, which, i).start()

    def inverse(t):
        x_copy(t).wait()
        total = jnp.zeros((rows, HD), f32)
        for c in range(width // HD):
            x = xrow[t, :, c * HD : (c + 1) * HD].astype(f32)
            total = total + x * x
        mean = jnp.sum(total, axis=1, keepdims=True) * (1.0 / width)
        invh[t, own_rows, :] = jnp.broadcast_to(lax.rsqrt(mean + EPS), (rows, HD))
        for d in range(1, n_tp):
            inv_send(t, d).start()

    for t in range(ticks):
        for which in range(2):
            send_kv(t, which)
        inverse(t)
        for d in range(1, n_tp):
            x_send(t, d).start()
        for d in range(1, n_tp):
            if t == 0:
                a_send(t, d).start()
            else:

                @pl.when(seg == last)
                def _(t=t, d=d):
                    a_send(t, d).start()

    def gain_of(g):
        return gain_ref[g : g + 1, :]

    def half_rows(h):
        return slice(h * HALF, (h + 1) * HALF)

    def head_cols(g):
        return slice(g * HD, (g + 1) * HD)

    def normed_of(t, h, g):
        return xh[t, half_rows(h), head_cols(g)].astype(f32) * invh[t, half_rows(h), :]

    def head_rows(g):
        return slice(g * HALF, (g + 1) * HALF)

    def prepare_queries(t, h):
        for g in range(group):
            qs[t, h, head_rows(g), :] = (normed_of(t, h, g) * gain_of(g)).astype(bf16)

    def prepare_arriving(t, h):
        for g in range(group):
            dos[h, head_rows(g), :] = ah[t, half_rows(h), head_cols(g)]

    unroll = pairs

    def each_group(step):
        @pl.loop(0, pairs // unroll)
        def _(i):
            step([i * unroll + u for u in range(unroll)])

    def half_of(p):
        return (p - low_pairs + n) // n

    def pair_of(t, p, which):
        return kv[t, pl.ds(2 * p, 2), which].reshape(2 * HALF, HD)

    chunks = [slice(c * chunk, (c + 1) * chunk) for c in range(lanes // chunk)]

    def wait_forwarded(t, which, p):
        h = half_of(p)

        @pl.when(2 * p + 1 < (1 - h) * (me + 1) + h * (high_first + n - me))
        def _():
            kv_wait(t, which, 2 * p + 1)

    def by_half(values, combine, empty):
        result = [jnp.full((1, lanes), empty, f32) for _ in range(2)]
        for p, value in enumerate(values):
            is_low = p < low_pairs
            result[0] = combine(result[0], jnp.where(is_low, value, empty))
            result[1] = combine(result[1], jnp.where(is_low, empty, value))
        return result

    def softmax(t):
        within = lax.rem(lax.broadcasted_iota(jnp.int32, (1, lanes), 1), HALF)
        low_pos = within + HALF * me
        low_start = jnp.zeros((1, lanes), jnp.int32)
        closing = jnp.int32(0)
        for k in range(docs):
            length = doc_ref[seg + t, k]
            closing = closing + length
            low_start = low_start + jnp.where(closing <= low_pos, length, 0)
        row = lax.broadcasted_iota(jnp.int32, (2 * HALF, chunk), 0)
        row = jnp.where(row < HALF, row, row - 2 * HALF)

        def step(group_pairs):
            for p in group_pairs:
                wait_forwarded(t, 0, p)
            for p in group_pairs:
                h = half_of(p)
                section = (1 - h) * me + h * (2 * n - 1 - me)
                base = HALF * (section - (2 * p - h * high_first))
                up_to = within + (HALF * section - base)
                down_to = jnp.where(h == 0, low_start, HALF * n) - base
                key_pair = pair_of(t, p, 0)
                for at in chunks:
                    s = dot_nt(key_pair, qs[t, h, at, :])
                    s = jnp.where((row <= up_to[:, at]) & (row >= down_to[:, at]), s, MASKED)
                    peak = jnp.max(s, axis=0, keepdims=True)
                    e = jnp.exp2((s - peak) * EXP2_SCALE)
                    m_ref[t, p, :, at] = peak
                    l_ref[p, :, at] = jnp.sum(e, axis=0, keepdims=True)
                    e_ref[t, p, :, at] = e

        each_group(step)
        peaks = [m_ref[t, p] for p in range(pairs)]
        peak = by_half(peaks, jnp.maximum, MASKED)
        alphas = [
            jnp.exp2((m - jnp.where(p < low_pairs, peak[0], peak[1])) * EXP2_SCALE)
            for p, m in enumerate(peaks)
        ]
        total = by_half([a * l_ref[p] for p, a in enumerate(alphas)], jnp.add, 0.0)
        inverse_total = [1.0 / part for part in total]
        for p, alpha in enumerate(alphas):
            m_ref[t, p] = alpha * jnp.where(p < low_pairs, inverse_total[0], inverse_total[1])

    def put_gradient(t, p, which, value):
        value = value.reshape(2, HALF, HD)
        gf[t, pl.ds(2 * p, 2), which] = value
        gb[t, pl.ds(2 * p, 2), which] = value.astype(bf16)

    def values_pass(t):
        def step(group_pairs):
            for p in group_pairs:
                wait_forwarded(t, 1, p)
            for p in group_pairs:
                h = half_of(p)
                value_pair = pair_of(t, p, 1)
                dv = jnp.zeros((2 * HALF, HD), f32)
                for at in chunks:
                    grads = dos[h, at, :]
                    probs = e_ref[t, p, :, at] * m_ref[t, p, :, at]
                    dp = dot_nt(value_pair, grads)
                    dv = dv + jnp.dot(probs.astype(bf16), grads, preferred_element_type=f32)
                    l_ref[p, :, at] = jnp.sum(probs * dp, axis=0, keepdims=True)
                    dp_ref[p, :, at] = dp
                put_gradient(t, p, 1, dv)

        each_group(step)
        terms = by_half([l_ref[p] for p in range(pairs)], jnp.add, 0.0)
        for h in range(2):
            rt_ref[h] = terms[h]

    def keys_pass(t):
        for h in range(2):
            dqt[h] = jnp.zeros((HD, lanes), f32)

        def step(group_pairs):
            for p in group_pairs:
                h = half_of(p)
                key_pair = pair_of(t, p, 0)
                dk = jnp.zeros((2 * HALF, HD), f32)
                for at in chunks:
                    probs = e_ref[t, p, :, at] * m_ref[t, p, :, at]
                    dscore = (probs * (dp_ref[p, :, at] - rt_ref[h, :, at])).astype(bf16)
                    dk = dk + jnp.dot(dscore, qs[t, h, at, :], preferred_element_type=f32)
                    dqt[h, :, at] += dot_tn(key_pair, dscore)
                put_gradient(t, p, 0, dk * SCALE)

        each_group(step)

    def partner_send(t, which, i):
        d = 2 * i + 1
        slot = slot_of(d)
        there = partner_slot(slot, upper(d))
        return remote(
            gb.at[t, slot, which],
            gp.at[t, there, which],
            gp_s.at[t, which, i],
            gp_r.at[t, which, there],
            {"ctx": partner},
        )

    def send_to_partner(t, which):
        @pl.loop(0, lines)
        def _(i):
            partner_send(t, which, i).start()

    def partner_wait(t, which, slot):
        came = gp.at[t, slot, which]
        remote(
            came, came, gp_s.at[t, which, 0], gp_r.at[t, which, slot], {"ctx": partner}
        ).wait_recv()

    def owner_send(t, which, i):
        return remote(
            gs.at[t, i, which],
            gz.at[t, i, which],
            gz_s.at[t, which, i],
            gz_r.at[t, which, i],
            {"ctx": ctx_behind(2 * i)},
        )

    def send_to_owners(t, which):
        for i in far_first:
            slot = slot_of(2 * i)
            partner_wait(t, which, slot)
            both = gf[t, slot, which] + gp[t, slot, which].astype(f32)
            gs[t, i, which] = both.astype(bf16)
            owner_send(t, which, i).start()

    def coupling_send(t, h, d):
        return remote(
            cs.at[t, h], cr.at[t, h, d], c_s.at[t, h, d], c_r.at[t, h, d], {"tp": tp_peer(d)}
        )

    diagonal = lax.broadcasted_iota(jnp.int32, (HALF, HD), 0) == lax.broadcasted_iota(
        jnp.int32, (HALF, HD), 1
    )

    def couple(t, h):
        dq = jnp.transpose(dqt[h] * SCALE)
        low = dq.astype(bf16)
        dqs[h] = low
        part = jnp.zeros((HALF, HD), f32)
        for g in range(group):
            rounded = low[g * HALF : (g + 1) * HALF, :].astype(f32)
            product = rounded * normed_of(t, h, g)
            gacc[pl.ds(g, 1), :] += jnp.sum(product, axis=0, keepdims=True)
            part = part + product * gain_of(g)
        part = jnp.sum(part, axis=1, keepdims=True)
        cs[t, h] = jnp.sum(jnp.where(diagonal, part, 0.0), axis=0, keepdims=True)
        for d in range(1, n_tp):
            coupling_send(t, h, d).start()

    def pipe_send(t, h):
        there = ah.at[t + 1, half_rows(h), :]
        return remote(
            ig.at[t, half_rows(h), :],
            there,
            p_s.at[t, h],
            p_r.at[t, h],
            {"pipe": lax.rem(seg + n_pipe - 1, n_pipe)},
        )

    def out_send(t, j):
        d = lax.rem(j + n_tp - tp, n_tp)
        return remote(
            ig.at[t, j * rows : (j + 1) * rows, :],
            ig_out.at[0, t, :, own_cols],
            o_s.at[t, d],
            o_r.at[t, d],
            {"tp": j},
        )

    def out_own(t):
        return pltpu.make_async_copy(
            ig.at[t, own_rows, :], ig_out.at[0, t, :, own_cols], o_s.at[t, 0]
        )

    per_half = n_tp // 2

    def finish(t, h):
        total = cs[t, h]
        for d in range(1, n_tp):
            coupling_send(t, h, d).wait_recv()
            total = total + cr[t, h, d]
        coupling = jnp.sum(jnp.where(diagonal, total, 0.0), axis=1, keepdims=True) * (1.0 / width)
        for g in range(group):
            normed = normed_of(t, h, g)
            scaled = dqs[h, g * HALF : (g + 1) * HALF, :].astype(f32) * gain_of(g)
            arriving = ah[t, half_rows(h), head_cols(g)].astype(f32)
            result = arriving + invh[t, half_rows(h), :] * (scaled - normed * coupling)
            ig[t, half_rows(h), head_cols(g)] = result.astype(bf16)
        if t + 1 < ticks:

            @pl.when(seg > 0)
            def _():
                pipe_send(t, h).start()

        for j in range(h * per_half, (h + 1) * per_half):

            @pl.when(tp != j)
            def _(j=j):
                out_send(t, j).start()

            @pl.when(tp == j)
            def _():
                out_own(t).start()

    gacc[...] = jnp.zeros((group, HD), f32)

    def wait_rows(t):
        own_x(t).wait()
        for d in range(1, n_tp):
            inv_send(t, d).wait_recv()
            x_send(t, d).wait_recv()

    def wait_arriving(t, h):
        if t == 0:
            if h == 0:
                own_a(t).wait()
                for d in range(1, n_tp):
                    a_send(t, d).wait_recv()
            return

        @pl.when(seg < last)
        def _():
            pipe_send(t - 1, h).wait_recv()

        if h == 0:

            @pl.when(seg == last)
            def _():
                own_output_grad(t).wait()
                for d in range(1, n_tp):
                    a_send(t, d).wait_recv()

    def queries(t):
        wait_rows(t)
        for h in range(2):
            prepare_queries(t, h)

    def values(t):
        for h in range(2):
            wait_arriving(t, h)
            prepare_arriving(t, h)
        values_pass(t)

    def gain_send(i):
        return remote(gacc, gr.at[i], g_s.at[i], g_r.at[i], {"ctx": ctx_peer(2 * i)})

    def gain_of_line():
        total = gacc[...]
        for i in range(1, lines):
            gain_send(i).wait_recv()
            total = total + gr[i]
        gr[0] = total
        gain_across.start()

    gain_across = remote(gr.at[0], gr.at[lines], g_s.at[0], g_r.at[0], {"ctx": partner})

    def gain_share(d):
        return remote(
            gr.at[lines + 1], gain_out.at[own_gain, :], h_s.at[d], h_r.at[d], {"tp": tp_peer(d)}
        )

    for which in range(2):
        forward_kv(0, which)
    for c in small_copies:
        c.wait()
    queries(0)
    softmax(0)
    for which in range(2):
        forward_kv(1, which)
    values(0)
    keys_pass(0)
    for h in range(2):
        couple(0, h)
    for which in range(2):
        send_to_partner(0, which)
    queries(1)
    for h in range(2):
        finish(0, h)
    softmax(1)
    for which in (1, 0):
        send_to_owners(0, which)
    values(1)
    send_to_partner(1, 1)
    keys_pass(1)
    send_to_partner(1, 0)
    for h in range(2):
        couple(1, h)

    for i in far_first:
        gain_send(i).start()
    send_to_owners(1, 1)
    for h in range(2):
        finish(1, h)
    send_to_owners(1, 0)
    gain_of_line()
    own_gain_copy = pltpu.make_async_copy(gr.at[lines + 1], gain_out.at[own_gain, :], h_s.at[0])

    def share_gain():
        gain_across.wait_recv()
        gr[lines + 1] = gr[0] + gr[lines]
        own_gain_copy.start()
        for d in range(1, n_tp):
            gain_share(d).start()

    def result_copy(t, which):
        out = (dk_out, dv_out)[which]
        return pltpu.make_async_copy(res.at[t, which], out.at[0, t], local_sem.at[t, which])

    for t in range(ticks):
        if t == ticks - 1:
            share_gain()
        for which in (1, 0):
            partner_wait(t, which, line * high_first)
            for i, mine in enumerate((0, high_first)):
                middle = (n + 1 - me) // 2
                begin, end = (1, middle) if i == 0 else (middle, lines)
                from_partner = jnp.where(line == i, gp[t, mine, which].astype(f32), 0.0)

                def add(k, total, t=t, which=which):
                    owner_send(t, which, k).wait_recv()
                    return total + gz[t, k, which].astype(f32)

                res[t, which, half_rows(i), :] = lax.fori_loop(
                    begin, end, add, gf[t, mine, which] + from_partner
                )
            result_copy(t, which).start()

    for t in range(ticks):
        for d in range(1, n_tp):
            inv_send(t, d).wait_send()
            x_send(t, d).wait_send()
            if t == 0:
                a_send(t, d).wait_send()
            else:

                @pl.when(seg == last)
                def _(t=t, d=d):
                    a_send(t, d).wait_send()

            for h in range(2):
                coupling_send(t, h, d).wait_send()

        for which in range(2):
            for i in range(lines):
                kv_forward(t, which, i).wait_send()
                if i > 0:
                    kv_send(t, which, i).wait_send()
                    owner_send(t, which, i).wait_send()

            @pl.loop(0, lines)
            def _(i, t=t, which=which):
                partner_send(t, which, i).wait_send()

            result_copy(t, which).wait()

        if t + 1 < ticks:
            for h in range(2):

                @pl.when(seg > 0)
                def _(t=t, h=h):
                    pipe_send(t, h).wait_send()

        for j in range(n_tp):

            @pl.when(tp != j)
            def _(t=t, j=j):
                out_send(t, j).wait_send()

            @pl.when(tp == j)
            def _(t=t):
                out_own(t).wait()

        for d in range(1, n_tp):
            came = ig_out.at[0, t, :, own_cols]
            remote(came, came, o_s.at[t, d], o_r.at[t, d], {"tp": tp_peer(d)}).wait_recv()
    for i in far_first:
        gain_send(i).wait_send()
    gain_across.wait_send()
    own_gain_copy.wait()

    for d in range(1, n_tp):
        gain_share(d).wait_send()
        gain_share(d).wait_recv()


def hand_over(*refs):
    *refs, sems = refs
    count = len(refs) // 3
    came, left, held = refs[:count], refs[count : 2 * count], refs[2 * count :]
    loads = [pltpu.make_async_copy(came[i], held[i], sems.at[0, i]) for i in range(count)]
    stores = [pltpu.make_async_copy(held[i], left[i], sems.at[1, i]) for i in range(count)]
    for c in loads:
        c.start()
    for load, store in zip(loads, stores):
        load.wait()
        store.start()
    for c in stores:
        c.wait()


def solution(mesh):
    n_pipe, n_ctx, n_tp = (mesh.shape[a] for a in ("pipe", "ctx", "tp"))

    def on_device(segment_inputs, keys, values, norm_gain, waiting_grads, output_grads, doc_lengths):
        ticks, rows, width = segment_inputs.shape[1:]
        cols = width // n_tp
        group = cols // HD
        docs = doc_lengths.shape[1]
        lanes = group * HALF
        slots = n_ctx + 2
        pairs = slots // 2
        dims = (n_pipe, n_ctx, n_tp, ticks, group, docs)
        dma = pltpu.SemaphoreType.DMA
        vmem = pltpu.VMEM
        hbm = pl.BlockSpec(memory_space=pl.ANY)
        lines = n_ctx // 2
        scratch = [
            vmem((ticks, rows, width), bf16),
            vmem((ticks, 2 * HALF, cols), bf16),
            vmem((ticks, 2 * HALF, cols), bf16),
            vmem((ticks, 2 * HALF, HD), f32),
            vmem((ticks, slots, 2, HALF, HD), bf16),
            vmem((ticks, 2, lanes, HD), bf16),
            vmem((2, lanes, HD), bf16),
            vmem((ticks, pairs, 2 * HALF, lanes), f32),
            vmem((pairs, 2 * HALF, lanes), f32),
            vmem((ticks, pairs, 1, lanes), f32),
            vmem((pairs, 1, lanes), f32),
            vmem((2, 1, lanes), f32),
            vmem((2, HD, lanes), f32),
            vmem((2, lanes, HD), bf16),
            vmem((ticks, slots, 2, HALF, HD), f32),
            vmem((ticks, slots, 2, HALF, HD), bf16),
            vmem((ticks, slots, 2, HALF, HD), bf16),
            vmem((ticks, lines, 2, HALF, HD), bf16),
            vmem((ticks, lines, 2, HALF, HD), bf16),
            vmem((ticks, 2 * HALF, cols), bf16),
            vmem((ticks, 2, 1, HD), f32),
            vmem((ticks, 2, n_tp, 1, HD), f32),
            vmem((group, HD), f32),
            vmem((lines + 2, group, HD), f32),
            vmem((ticks, 2, 2 * HALF, HD), f32),
            vmem((group, HD), f32),
            pltpu.SMEM(doc_lengths.shape, jnp.int32),
            dma((ticks, 7)),
            dma((2,)),
            dma((ticks, n_tp)),
            dma((ticks, n_tp)),
            dma((ticks, n_tp)),
            dma((ticks, n_tp)),
            dma((ticks, n_tp)),
            dma((ticks, n_tp)),
            dma((ticks, 2, lines)),
            dma((ticks, 2, slots)),
            dma((ticks, 2, lines)),
            dma((ticks, 2, lines)),
            dma((ticks, 2, slots)),
            dma((ticks, 2, lines)),
            dma((ticks, 2, lines)),
            dma((ticks, 2, n_tp)),
            dma((ticks, 2, n_tp)),
            dma((ticks, 2)),
            dma((ticks, 2)),
            dma((ticks, n_tp)),
            dma((ticks, n_tp)),
            dma((lines,)),
            dma((lines,)),
            dma((n_tp,)),
            dma((n_tp,)),
        ]
        input_grads, key_grads, value_grads, gain_grads = pl.pallas_call(
            functools.partial(kernel, dims),
            out_shape=(
                jax.ShapeDtypeStruct((1, ticks, rows, width), bf16),
                jax.ShapeDtypeStruct((1, ticks, 2 * HALF, HD), f32),
                jax.ShapeDtypeStruct((1, ticks, 2 * HALF, HD), f32),
                jax.ShapeDtypeStruct((width // HD, HD), f32),
            ),
            in_specs=[
                hbm,
                hbm,
                hbm,
                hbm,
                hbm,
                hbm,
                hbm,
            ],
            out_specs=(hbm,) * 4,
            scratch_shapes=scratch,
            compiler_params=pltpu.CompilerParams(
                collective_id=0, has_side_effects=True, vmem_limit_bytes=KERNEL_VMEM
            ),
            name="window",
        )(
            segment_inputs,
            keys,
            values,
            norm_gain.reshape(width // HD, HD),
            waiting_grads,
            output_grads,
            doc_lengths,
        )
        made = (input_grads, key_grads, value_grads, gain_grads)
        input_grads, key_grads, value_grads, gain_grads = pl.pallas_call(
            hand_over,
            out_shape=tuple(jax.ShapeDtypeStruct(a.shape, a.dtype) for a in made),
            in_specs=[hbm] * len(made),
            out_specs=(hbm,) * len(made),
            scratch_shapes=[vmem(a.shape, a.dtype) for a in made] + [dma((2, len(made)))],
            compiler_params=pltpu.CompilerParams(vmem_limit_bytes=KERNEL_VMEM),
            name="hand_over",
        )(*made)
        return input_grads, key_grads, value_grads, gain_grads.reshape(1, width)

    in_specs = (
        P("pipe", None, ("ctx", "tp"), None),
        P("pipe", None, "ctx", "tp"),
        P("pipe", None, "ctx", "tp"),
        P("pipe", None),
        P("pipe", ("ctx", "tp"), None),
        P(None, ("ctx", "tp"), None),
        P(),
    )
    out_specs = (
        P("pipe", None, ("ctx", "tp"), None),
        P("pipe", None, "ctx", "tp"),
        P("pipe", None, "ctx", "tp"),
        P("pipe", None),
    )
    return jax.shard_map(
        on_device, mesh=mesh, in_specs=in_specs, out_specs=out_specs, check_vma=False
    )
```
